256 devices in a mesh: layer: 2 (over core), prow: 4 (over x), pcol: 32 (over y, z).
Axes of the slice: x: 4, y: 4, z: 8, core: 2. Of those that a mesh axis runs over, the one named last changes fastest.
Arguments:
- right_sub: float32 [14, 64, 4096], P('layer', None, 'prow'), may hold values from -3 to 3
- right_root: float32 [64, 4096], P(None, 'prow'), may hold values from -3 to 3
- inverse_sub: bfloat16 [14, 4096, 4096], P('layer', 'prow', 'pcol'), as said below
- inverse_root: bfloat16 [4096, 4096], P('prow', 'pcol')
- factor_blocks: bfloat16 [34, 4096, 2048], P('layer', 'pcol', 'prow'), may hold values from -0.046875 to 0.046875
- block_lists: int32 [34, 8], P('layer', 'prow'), may hold values from 0 to 15, all different within a row
Outputs:
- solution_sub: float32 [14, 64, 4096], P('layer', None, 'prow')
- solution_root: float32 [64, 4096], P(None, 'prow')
The draws below stay inside these ranges and needn't reach their ends.
Inputs may be any that keep to these rules, and one draw needn't show every extreme that they name: `block_lists`: each row names 8 different block rows of its ancestor. inverse_sub and inverse_root are upper triangular (the transpose of a lower-triangular inverse, zero below the diagonal) and well conditioned.
All inputs are finite; a program needn't handle non-finite values.
Results may differ from the reference program's by a relative error of at most 0.009.
Values may be sent and summed in bfloat16 or wider, within the bound.
No kernel may reach another device: no remote copies, remote signals or barrier semaphores. Data moves between devices by JAX's collectives and lax.ppermute only.
A program may use at most 128 MiB of HBM per device.

```python
import math
import jax
import jax.numpy as jnp
from jax import lax

W = 256
NB = 16
RHS = 64
NODES = 7
PAIRS = 17
NR = 8
M = 4096


def identity_plus(noise):
    size_rows = noise.shape[-1]
    first_index = lax.broadcasted_iota(jnp.int32, noise.shape, noise.ndim - 2)
    second_index = lax.broadcasted_iota(jnp.int32, noise.shape, noise.ndim - 1)
    diagonal_mask = (first_index == second_index).astype(jnp.float32)
    upper_mask = (second_index >= first_index).astype(jnp.float32)
    return (diagonal_mask + noise * (0.45 / math.sqrt(size_rows))) * upper_mask


def draw_inverse_sub(key, part):
    shape_full = (2 * NODES, M, M)
    noise = jax.random.normal(key, shape_full, jnp.float32)
    return identity_plus(noise).astype(jnp.bfloat16)


def draw_inverse_root(key, part):
    own_key = jax.random.fold_in(key, 11)
    shape_full = (M, M)
    noise = jax.random.normal(own_key, shape_full, jnp.float32)
    return identity_plus(noise).astype(jnp.bfloat16)


def block_levels(key, dims, shards, least, top_value):
    factor_of = 1.0
    for position, shards_of in shards:
        heights = jax.random.uniform(jax.random.fold_in(jax.random.fold_in(key, 6), position), (shards_of,), jnp.float32, least / len(shards), top_value / len(shards))
        factor_of = factor_of * jnp.repeat(jnp.exp(heights), dims[position] // shards_of).reshape((-1,) + (1,) * (len(dims) - 1 - position))
    return factor_of


def picks_of(rng, rows, count, top, lift):
    ranking = jax.random.permutation(jax.random.fold_in(rng, 1), count)
    favour = ranking
    for power in range(3):
        favour = favour * favour // count
    favour = favour * lift // count
    lots = jax.random.randint(jax.random.fold_in(rng, 2), (rows, count), 0, 4096) + favour
    sure = jax.random.permutation(jax.random.fold_in(rng, 3), rows)[jnp.arange(count) % rows]
    lots = jnp.where(jnp.arange(rows)[:, None] == sure[None, :], 1 << 14, lots)
    score = lots * count + jnp.arange(count)
    return lax.top_k(score.astype(jnp.int32), top)[1].astype(jnp.int32)


def gaussian(key, shape, scale, most, cuts=(), kind=jnp.bfloat16):
    values = jax.random.normal(key, shape, jnp.float32) * scale
    if len(cuts) > 0:
        values = block_levels(key, shape, cuts, -0.22, 0.18) * values
    return jnp.clip(values, min=-most, max=most).astype(kind)


def setup_inputs(seed: int = 0) -> dict:
    splits = jax.random.split(jax.random.key(seed), 7)
    right_sub = gaussian(splits[0], (2 * NODES, RHS, M), 0.5, 3.0, ((0, 2), (2, 4)), jnp.float32)
    right_root = gaussian(splits[1], (RHS, M), 0.5, 3.0, ((1, 4),), jnp.float32)
    inverse_sub = draw_inverse_sub(jax.random.fold_in(splits[6], 71), 0)
    inverse_root = draw_inverse_root(jax.random.fold_in(splits[6], 71), 0)
    factor_blocks = gaussian(splits[4], (2 * PAIRS, M, NR * W), (4 * M) ** -0.5, 0.046875, ((0, 2), (1, 32), (2, 4)))
    block_lists = picks_of(splits[5], (2 * PAIRS), NB, NR, 8192)
    return dict(right_sub=right_sub, right_root=right_root, inverse_sub=inverse_sub, inverse_root=inverse_root, factor_blocks=factor_blocks, block_lists=block_lists)


def tree_pairs():
    listing = []
    for node_index in range(NODES):
        ancestry = []
        walker = node_index
        while walker > 0:
            walker = (walker - 1) // 2
            ancestry.append(walker)
        listing.append((node_index, -1))
        for above in reversed(ancestry):
            listing.append((node_index, above))
    return listing


def level_range(level_now):
    return 2 ** (level_now - 1) - 1, 2 ** level_now - 1


def spread_blocks(update, selector):
    blocked = update.reshape(RHS, NR, W)
    spread = jnp.einsum("rkw,kn->rnw", blocked, selector, precision=lax.Precision.HIGHEST)
    return spread.reshape(RHS, NB * W)


def pick_blocks(values, selector):
    blocked = values.astype(jnp.float32).reshape(RHS, NB, W)
    picked = jnp.einsum("rnw,kn->rkw", blocked, selector, precision=lax.Precision.HIGHEST)
    return picked.reshape(RHS, NR * W).astype(jnp.bfloat16)


def reference(right_sub, right_root, inverse_sub, inverse_root, factor_blocks, block_lists):
    listing = tree_pairs()
    selectors = (block_lists[:, :, None] == jnp.arange(NB, dtype=jnp.int32)[None, None, :]).astype(jnp.float32)
    pending = {}
    for layer_index in range(2):
        for node_index in range(NODES):
            pending[(layer_index, node_index)] = jnp.zeros((RHS, M), jnp.float32)
    pending_root = jnp.zeros((RHS, M), jnp.float32)
    forward_values = {}
    for level_now in (3, 2, 1):
        first_node, last_node = level_range(level_now)
        for layer_index in range(2):
            for node_index in range(first_node, last_node):
                stored = layer_index * NODES + node_index
                residual = right_sub[stored] - pending[(layer_index, node_index)]
                solved = jnp.dot(residual.astype(jnp.bfloat16), inverse_sub[stored], preferred_element_type=jnp.float32)
                forward_values[(layer_index, node_index)] = solved
                rounded = solved.astype(jnp.bfloat16)
                for pair_index, (owner, above) in enumerate(listing):
                    if owner == node_index:
                        placed = layer_index * PAIRS + pair_index
                        update = jnp.dot(rounded, factor_blocks[placed], preferred_element_type=jnp.float32)
                        spread = spread_blocks(update, selectors[placed])
                        if above < 0:
                            pending_root = pending_root + spread
                        else:
                            pending[(layer_index, above)] = pending[(layer_index, above)] + spread
    root_forward = jnp.dot((right_root - pending_root).astype(jnp.bfloat16), inverse_root, preferred_element_type=jnp.float32)
    solution_root = jnp.dot(root_forward.astype(jnp.bfloat16), inverse_root.T, preferred_element_type=jnp.float32)
    full_values = {}
    for layer_index in range(2):
        full_values[(layer_index, -1)] = solution_root.astype(jnp.bfloat16)
    solutions = [None] * (2 * NODES)
    for level_now in (1, 2, 3):
        first_node, last_node = level_range(level_now)
        for layer_index in range(2):
            for node_index in range(first_node, last_node):
                stored = layer_index * NODES + node_index
                total = jnp.zeros((RHS, M), jnp.float32)
                for pair_index, (owner, above) in enumerate(listing):
                    if owner == node_index:
                        placed = layer_index * PAIRS + pair_index
                        picked = pick_blocks(full_values[(layer_index, above)], selectors[placed])
                        total = total + jnp.dot(picked, factor_blocks[placed].T, preferred_element_type=jnp.float32)
                target = forward_values[(layer_index, node_index)] - total
                solution = jnp.dot(target.astype(jnp.bfloat16), inverse_sub[stored].T, preferred_element_type=jnp.float32)
                solutions[stored] = solution
                full_values[(layer_index, node_index)] = solution.astype(jnp.bfloat16)
    return jnp.stack(solutions), solution_root
```

```python
import jax
import jax.numpy as jnp
from jax import lax
from jax.experimental import pallas as pl
from jax.experimental.pallas import tpu as pltpu
from jax.sharding import PartitionSpec as P

NX = 4
NP = 32
RX = 16
BF = jnp.bfloat16
F32 = jnp.float32
LIMIT = 56 * 1024 * 1024

SMEM = pl.BlockSpec(memory_space=pltpu.SMEM)


def params():
    return pltpu.CompilerParams(vmem_limit_bytes=LIMIT)


def shift(value, distance):
    return lax.ppermute(value, "prow", [(i, (i + distance) % NX) for i in range(NX)])


def around(value):
    return [value] + [shift(value, distance) for distance in range(1, NX)]


def after(value, *earlier):
    return lax.optimization_barrier((value, *earlier))[0]


def exchange(value):
    return lax.all_to_all(value, "pcol", 0, 0, tiled=True)


def reduce_columns(parts):
    return jnp.sum(exchange(parts).astype(F32), axis=0)


def gather_columns(chunk):
    chunk = chunk.astype(BF)
    return exchange(jnp.broadcast_to(chunk[None], (NP,) + chunk.shape))


def dot(left, right):
    return lax.dot_general(left, right, (((1,), (0,)), ((), ())), preferred_element_type=F32)


def dot_t(left, right):
    return lax.dot_general(left, right, (((1,), (1,)), ((), ())), preferred_element_type=F32)


def row_start(x, distance):
    return pl.multiple_of(lax.rem(x + distance, NX) * RX, RX)


def source(x, distance):
    return lax.rem(x + (NX - distance), NX)


def leaf_update_kernel(x_ref, own, r1, r2, r3, factor, fwd, *rest):
    crit, other, total = rest[0:4], rest[4:8], rest[8]
    x = x_ref[0]
    total[...] = (own[...].astype(F32) + r1[...].astype(F32)) + (
        r2[...].astype(F32) + r3[...].astype(F32)
    )
    for n in range(4):
        fwd[n] = total[n, pl.ds(row_start(x, 0), RX), :]
        left = jnp.concatenate(
            [total[n, pl.ds(row_start(x, d), RX), :] for d in range(NX)], axis=0
        ).astype(BF)
        for i in range(3):
            update = dot(left, factor[3 * n + i]).astype(BF)
            for d in range(NX):
                piece = update[RX * d : RX * (d + 1)]
                if i == 2:
                    crit[d][n] = piece
                else:
                    other[d][2 * n + i] = piece


def leaf_update(x, own, received, factor):
    out = (
        [jax.ShapeDtypeStruct((4, RX, 128), F32)]
        + [jax.ShapeDtypeStruct((4, RX, 512), BF)] * 4
        + [jax.ShapeDtypeStruct((8, RX, 512), BF)] * 4
    )
    result = pl.pallas_call(
        leaf_update_kernel,
        out_shape=out,
        in_specs=[SMEM] + [pl.BlockSpec(memory_space=pltpu.VMEM)] * 5,
        scratch_shapes=[pltpu.VMEM((4, 64, 128), F32)],
        compiler_params=params(),
        name="leaf_update",
    )(x, own, *received, factor)
    return result[0], result[1:5], result[5:9]


def add_update(acc, lists, distance, pair, update, *lead):
    for j in range(2):
        block = lists[distance][pair, j]
        for h in range(2):
            index = (2 * block + h, *lead)
            tile = update[:, 256 * j + 128 * h : 256 * j + 128 * (h + 1)]
            acc[index] = acc[index] + tile.astype(F32)


def leaf_spread_kernel(l0, l1, l2, l3, c0, c1, c2, c3, out, acc):
    lists = (l0, l1, l2, l3)
    acc[...] = jnp.zeros(acc.shape, F32)
    for d, crit in enumerate((c0, c1, c2, c3)):
        for n in range(4):
            add_update(acc, lists, d, 5 + 3 * n + 2, crit[n], n // 2)
    out[...] = acc[...].astype(BF)


def leaf_spread(lists, crit):
    return pl.pallas_call(
        leaf_spread_kernel,
        out_shape=jax.ShapeDtypeStruct((NP, 2, RX, 128), BF),
        in_specs=[SMEM] * 4 + [pl.BlockSpec(memory_space=pltpu.VMEM)] * 4,
        scratch_shapes=[pltpu.VMEM((NP, 2, RX, 128), F32)],
        compiler_params=params(),
        name="leaf_spread",
    )(*lists, *crit)


def solve_columns(x, values, inverses, which, *lead):
    total = None
    for d in range(NX):
        first = 8 * source(x, d)
        left = jnp.concatenate([values[(first + k, *lead)] for k in range(8)], axis=1)
        term = dot(left, inverses[d][which])
        total = term if total is None else total + term
    return total


def solve_rows(x, target, inverses, which, store):
    for d in range(NX):
        row = source(x, d)
        wide = dot_t(target, inverses[d][which]).astype(BF)
        for k in range(8):
            store(row, k, wide[:, 128 * k : 128 * (k + 1)])


def pick_product(lists, pair, local_pair, values, factors, *lead):
    total = None
    for d in range(NX):
        tiles = []
        for j in range(2):
            block = lists[d][pair, j]
            tiles += [values[(2 * block, *lead)], values[(2 * block + 1, *lead)]]
        term = dot_t(jnp.concatenate(tiles, axis=1), factors[d][local_pair])
        total = term if total is None else total + term
    return total


def middle_forward_kernel(x_ref, *refs):
    lists, values, inverses, factors, other = (
        refs[0:4], refs[4], refs[5:9], refs[9:13], refs[13:17],
    )
    fwd, out, acc_root, acc = refs[17:21]
    x = x_ref[0]
    acc[...] = jnp.zeros(acc.shape, F32)
    acc_root[...] = jnp.zeros(acc_root.shape, F32)
    for d in range(NX):
        for n in range(4):
            add_update(acc_root, lists, d, 5 + 3 * n, other[d][2 * n])
            add_update(acc, lists, d, 5 + 3 * n + 1, other[d][2 * n + 1])
    for m in range(2):
        solved = solve_columns(x, values, inverses, m, m)
        fwd[m] = solved
        rounded = solved.astype(BF)
        for d in range(NX):
            add_update(acc_root, lists, d, 1 + 2 * m, dot(rounded, factors[d][1 + 2 * m]))
            add_update(acc, lists, d, 2 + 2 * m, dot(rounded, factors[d][2 + 2 * m]))
    out[...] = acc[...].astype(BF)


def middle_forward(x, lists, values, inverses, factors, other):
    return pl.pallas_call(
        middle_forward_kernel,
        out_shape=[
            jax.ShapeDtypeStruct((2, RX, 128), F32),
            jax.ShapeDtypeStruct((NP, RX, 128), BF),
            jax.ShapeDtypeStruct((NP, RX, 128), F32),
        ],
        in_specs=[SMEM] * 5 + [pl.BlockSpec(memory_space=pltpu.VMEM)] * 13,
        scratch_shapes=[pltpu.VMEM((NP, RX, 128), F32)],
        compiler_params=params(),
        name="middle_forward",
    )(x, *lists, values, *inverses, *factors, *other)


def top_forward_kernel(x_ref, *refs):
    lists, values, inverses, factors, acc_in = refs[0:4], refs[4], refs[5:9], refs[9:13], refs[13]
    fwd, out, acc = refs[14:17]
    x = x_ref[0]
    acc[...] = acc_in[...]
    solved = solve_columns(x, values, inverses, 0)
    fwd[...] = solved
    rounded = solved.astype(BF)
    for d in range(NX):
        add_update(acc, lists, d, 0, dot(rounded, factors[d][0]))
    out[...] = acc[...].astype(BF)


FIRST_PAIR = pl.BlockSpec((1, 128, 512), lambda i: (0, 0, 0))


def top_forward(x, lists, values, inverses, factors, acc_root):
    return pl.pallas_call(
        top_forward_kernel,
        grid=(1,),
        out_shape=[
            jax.ShapeDtypeStruct((RX, 128), F32),
            jax.ShapeDtypeStruct((NP, RX, 128), BF),
        ],
        in_specs=[SMEM] * 5
        + [pl.BlockSpec((NP, RX, 128), lambda i: (0, 0, 0))]
        + [pl.BlockSpec((1, 1024, 128), lambda i: (0, 0, 0))] * 4
        + [FIRST_PAIR] * 4
        + [pl.BlockSpec((NP, RX, 128), lambda i: (0, 0, 0))],
        out_specs=[
            pl.BlockSpec((RX, 128), lambda i: (0, 0)),
            pl.BlockSpec((NP, RX, 128), lambda i: (0, 0, 0)),
        ],
        scratch_shapes=[pltpu.VMEM((NP, RX, 128), F32)],
        compiler_params=params(),
        name="top_forward",
    )(x, *lists, values, *inverses, *factors, acc_root)


def root_kernel(x_ref, values, i0, i1, i2, i3, out):
    x = x_ref[0]
    inverses = (i0, i1, i2, i3)
    rounded = solve_columns(x, values, inverses, 0).astype(BF)

    def store(row, k, tile):
        out[8 * row + k] = tile

    solve_rows(x, rounded, inverses, 0, store)


def root_solve(x, values, inverses):
    return pl.pallas_call(
        root_kernel,
        grid=(1,),
        out_shape=jax.ShapeDtypeStruct((NP, RX, 128), BF),
        in_specs=[SMEM]
        + [pl.BlockSpec((NP, RX, 128), lambda i: (0, 0, 0))]
        + [pl.BlockSpec((1, 1024, 128), lambda i: (1, 0, 0))] * 4,
        out_specs=pl.BlockSpec((NP, RX, 128), lambda i: (0, 0, 0)),
        compiler_params=params(),
        name="root_solve",
    )(x, values, *inverses)


def top_backward_kernel(x_ref, *refs):
    lists, root, fwd, inverses, factors, out = (
        refs[0:4], refs[4], refs[5], refs[6:10], refs[10:14], refs[14],
    )
    x = x_ref[0]
    target = (fwd[...] - pick_product(lists, 0, 0, root, factors)).astype(BF)

    def store(row, k, tile):
        out[8 * row + k] = tile

    solve_rows(x, target, inverses, 0, store)


def top_backward(x, lists, root, fwd, inverses, factors):
    return pl.pallas_call(
        top_backward_kernel,
        grid=(1,),
        out_shape=jax.ShapeDtypeStruct((NP, RX, 128), BF),
        in_specs=[SMEM] * 5
        + [pl.BlockSpec((NP, RX, 128), lambda i: (0, 0, 0)), pl.BlockSpec((RX, 128), lambda i: (0, 0))]
        + [pl.BlockSpec((1, 1024, 128), lambda i: (0, 0, 0))] * 4
        + [FIRST_PAIR] * 4,
        out_specs=pl.BlockSpec((NP, RX, 128), lambda i: (0, 0, 0)),
        compiler_params=params(),
        name="top_backward",
    )(x, *lists, root, fwd, *inverses, *factors)


def middle_backward_kernel(x_ref, *refs):
    lists, root, top, fwd, inverses, factors, out = (
        refs[0:4], refs[4], refs[5], refs[6], refs[7:11], refs[11:15], refs[15],
    )
    x = x_ref[0]
    for m in range(2):
        down = pick_product(lists, 1 + 2 * m, 1 + 2 * m, root, factors)
        down = down + pick_product(lists, 2 + 2 * m, 2 + 2 * m, top, factors)
        target = (fwd[m] - down).astype(BF)

        def store(row, k, tile, m=m):
            out[8 * row + k, m] = tile

        solve_rows(x, target, inverses, m, store)


def middle_backward(x, lists, root, top, fwd, inverses, factors):
    return pl.pallas_call(
        middle_backward_kernel,
        out_shape=jax.ShapeDtypeStruct((NP, 2, RX, 128), BF),
        in_specs=[SMEM] * 5 + [pl.BlockSpec(memory_space=pltpu.VMEM)] * 11,
        compiler_params=params(),
        name="middle_backward",
    )(x, *lists, root, top, fwd, *inverses, *factors)


def leaf_backward_kernel(x_ref, *refs):
    lists, root, top, middle, fwd, inverses, factors, out = (
        refs[0:4], refs[4], refs[5], refs[6], refs[7], refs[8:12], refs[12:16], refs[16],
    )
    x = x_ref[0]
    n = pl.program_id(0)
    first = 5 + 3 * n
    down = pick_product(lists, first, 0, root, factors)
    down = down + pick_product(lists, first + 1, 1, top, factors)
    down = down + pick_product(lists, first + 2, 2, middle, factors, n // 2)
    target = (fwd[0] - down).astype(BF)

    def store(row, k, tile):
        out[k, row] = tile

    solve_rows(x, target, inverses, 0, store)


def leaf_backward(x, lists, root, top, middle, fwd, inverses, factors):
    whole = lambda shape: pl.BlockSpec(shape, lambda n: (0,) * len(shape))
    return pl.pallas_call(
        leaf_backward_kernel,
        grid=(4,),
        out_shape=jax.ShapeDtypeStruct((NP, NX, RX, 128), BF),
        in_specs=[SMEM] * 5
        + [whole((NP, RX, 128)), whole((NP, RX, 128)), whole((NP, 2, RX, 128))]
        + [pl.BlockSpec((1, RX, 128), lambda n: (n, 0, 0))]
        + [pl.BlockSpec((1, 1024, 128), lambda n: (n, 0, 0))] * 4
        + [pl.BlockSpec((3, 128, 512), lambda n: (n, 0, 0))] * 4,
        out_specs=pl.BlockSpec((8, NX, RX, 128), lambda n: (n, 0, 0, 0)),
        compiler_params=params(),
        name="leaf_backward",
    )(x, *lists, root, top, middle, fwd, *inverses, *factors)


def finish_kernel(x_ref, e0, e1, e2, e3, leaves, out_sub, out_root):
    x = x_ref[0]
    for d, early in enumerate((e0, e1, e2, e3)):
        rows = pl.ds(pl.multiple_of(RX * source(x, d), RX), RX)
        for k in range(8):
            columns = slice(128 * k, 128 * (k + 1))
            out_root[rows, columns] = early[k, 0].astype(F32)
            for t in range(3):
                out_sub[t, rows, columns] = early[k, 1 + t].astype(F32)
    for t in range(4):
        for k in range(8):
            out_sub[3 + t, :, 128 * k : 128 * (k + 1)] = leaves[8 * t + k].astype(F32)


def finish(x, early, leaves):
    return pl.pallas_call(
        finish_kernel,
        out_shape=[
            jax.ShapeDtypeStruct((7, 64, 1024), F32),
            jax.ShapeDtypeStruct((64, 1024), F32),
        ],
        in_specs=[SMEM] + [pl.BlockSpec(memory_space=pltpu.VMEM)] * 5,
        compiler_params=params(),
        name="finish",
    )(x, *early, leaves)


def per_device(right_sub, right_root, inverse_sub, inverse_root, factor_blocks, block_lists):
    position = lax.axis_index("prow")
    column = lax.axis_index("pcol")
    x = position.astype(jnp.int32)[None]

    inverse_leaf = inverse_sub[3:7]
    factor_leaf = factor_blocks[5:17]
    own = jnp.einsum(
        "nrm,nmc->nrc", right_sub[3:7].astype(BF), inverse_leaf, preferred_element_type=F32
    ).astype(BF)
    received = around(own)
    lists = around(block_lists)

    def right_piece(d):
        row = RX * lax.rem(position + d, NX)
        start = 128 * lax.rem(column, 8)
        sub = lax.dynamic_slice(right_sub, (0, row, start), (3, RX, 128))
        root = lax.dynamic_slice(right_root, (row, start), (RX, 128))
        return jnp.concatenate([sub, root[None]], 0)

    right = right_piece(0)
    held = lax.rem(position + NX - column // 8, NX)
    for d in range(1, NX):
        right = jnp.where(held == d, shift(right_piece(d), d), right)

    fwd_leaf, crit, other = leaf_update(x, own, received[1:], factor_leaf)
    crit = [crit[0]] + [shift(crit[d], d) for d in range(1, NX)]
    other = [other[0]] + [shift(other[d], d) for d in range(1, NX)]

    inverse_middle = around(inverse_sub[1:3])
    factor_upper = around(factor_blocks[0:5])
    inverse_top = around(jnp.concatenate([inverse_sub[0:1], inverse_root[None]], 0))

    parts = leaf_spread(lists, crit)
    values = gather_columns(right[1:3] - reduce_columns(parts))
    inverse_leaf = around(after(inverse_leaf, values))
    factor_leaf = around(after(factor_leaf, values))

    fwd_middle, parts, acc_root = middle_forward(x, lists, values, inverse_middle, factor_upper, other)
    values = gather_columns(right[0] - reduce_columns(parts))
    fwd_top, parts = top_forward(x, lists, values, inverse_top, factor_upper, acc_root)
    total = reduce_columns(parts)
    total = total + lax.ppermute(total, "layer", [(0, 1), (1, 0)])
    values = gather_columns(right[3] - total)
    root = gather_columns(reduce_columns(root_solve(x, values, inverse_top)))
    top = gather_columns(
        reduce_columns(top_backward(x, lists, root, fwd_top, inverse_top, factor_upper))
    )
    middle = gather_columns(
        reduce_columns(
            middle_backward(x, lists, root, top, fwd_middle, inverse_middle, factor_upper)
        )
    )

    early = jnp.concatenate([root[:, None], top[:, None], middle], 1)
    pieces = []
    for d in range(NX):
        piece = lax.dynamic_slice_in_dim(early, 8 * lax.rem(position + d, NX), 8, 0)
        pieces.append(shift(piece, d) if d else piece)

    parts = leaf_backward(x, lists, root, top, middle, fwd_leaf, inverse_leaf, factor_leaf)
    chunk = reduce_columns(parts).astype(BF)
    chunk = lax.all_to_all(chunk, "prow", 0, 0, tiled=True).reshape(4 * RX, 128)
    leaves = gather_columns(chunk)
    return tuple(finish(x, pieces, leaves))


def solution(mesh):
    in_specs = (
        P("layer", None, "prow"),
        P(None, "prow"),
        P("layer", "prow", "pcol"),
        P("prow", "pcol"),
        P("layer", "pcol", "prow"),
        P("layer", "prow"),
    )
    out_specs = (P("layer", None, "prow"), P(None, "prow"))
    return jax.shard_map(
        per_device, mesh=mesh, in_specs=in_specs, out_specs=out_specs, check_vma=False
    )
```

```python
import jax
import jax.numpy as jnp
from jax import lax
from jax.experimental import pallas as pl
from jax.experimental.pallas import tpu as pltpu
from jax.sharding import PartitionSpec as P

NX = 4
NP = 32
RX = 16
BF = jnp.bfloat16
F32 = jnp.float32
LIMIT = 56 * 1024 * 1024

SMEM = pl.BlockSpec(memory_space=pltpu.SMEM)


def params():
    return pltpu.CompilerParams(vmem_limit_bytes=LIMIT)


def shift(value, distance):
    return lax.ppermute(value, "prow", [(i, (i + distance) % NX) for i in range(NX)])


def around(value):
    return [value] + [shift(value, distance) for distance in range(1, NX)]


def after(value, *earlier):
    return lax.optimization_barrier((value, *earlier))[0]


def exchange(value):
    return lax.all_to_all(value, "pcol", 0, 0, tiled=True)


def reduce_columns(parts):
    return jnp.sum(exchange(parts).astype(F32), axis=0)


def gather_columns(chunk):
    chunk = chunk.astype(BF)
    return exchange(jnp.broadcast_to(chunk[None], (NP,) + chunk.shape))


def dot(left, right):
    return lax.dot_general(left, right, (((1,), (0,)), ((), ())), preferred_element_type=F32)


def dot_t(left, right):
    return lax.dot_general(left, right, (((1,), (1,)), ((), ())), preferred_element_type=F32)


def row_start(x, distance):
    return pl.multiple_of(lax.rem(x + distance, NX) * RX, RX)


def source(x, distance):
    return lax.rem(x + (NX - distance), NX)


def leaf_update_kernel(x_ref, own, r1, r2, r3, factor, fwd, *rest):
    crit, other, total = rest[0:4], rest[4:8], rest[8]
    x = x_ref[0]
    total[...] = (own[...].astype(F32) + r1[...].astype(F32)) + (
        r2[...].astype(F32) + r3[...].astype(F32)
    )
    for n in range(4):
        fwd[n] = total[n, pl.ds(row_start(x, 0), RX), :]
        left = jnp.concatenate(
            [total[n, pl.ds(row_start(x, d), RX), :] for d in range(NX)], axis=0
        ).astype(BF)
        for i in range(3):
            update = dot(left, factor[3 * n + i]).astype(BF)
            for d in range(NX):
                piece = update[RX * d : RX * (d + 1)]
                if i == 2:
                    crit[d][n] = piece
                else:
                    other[d][2 * n + i] = piece


def leaf_update(x, own, received, factor):
    out = (
        [jax.ShapeDtypeStruct((4, RX, 128), F32)]
        + [jax.ShapeDtypeStruct((4, RX, 512), BF)] * 4
        + [jax.ShapeDtypeStruct((8, RX, 512), BF)] * 4
    )
    result = pl.pallas_call(
        leaf_update_kernel,
        out_shape=out,
        in_specs=[SMEM] + [pl.BlockSpec(memory_space=pltpu.VMEM)] * 5,
        scratch_shapes=[pltpu.VMEM((4, 64, 128), F32)],
        compiler_params=params(),
        name="leaf_update",
    )(x, own, *received, factor)
    return result[0], result[1:5], result[5:9]


def listed(table, distance, pair, j):
    return table[(distance * 17 + pair) * 2 + j]


def add_update(acc, table, distance, pair, update, *lead):
    for j in range(2):
        block = listed(table, distance, pair, j)
        for h in range(2):
            index = (2 * block + h, *lead)
            tile = update[:, 256 * j + 128 * h : 256 * j + 128 * (h + 1)]
            acc[index] = acc[index] + tile.astype(F32)


def leaf_spread_kernel(lists, c0, c1, c2, c3, out, acc):
    acc[...] = jnp.zeros(acc.shape, F32)
    for d, crit in enumerate((c0, c1, c2, c3)):
        for n in range(4):
            add_update(acc, lists, d, 5 + 3 * n + 2, crit[n], n // 2)
    out[...] = acc[...].astype(BF)


def leaf_spread(lists, crit):
    return pl.pallas_call(
        leaf_spread_kernel,
        out_shape=jax.ShapeDtypeStruct((NP, 2, RX, 128), BF),
        in_specs=[SMEM] + [pl.BlockSpec(memory_space=pltpu.VMEM)] * 4,
        scratch_shapes=[pltpu.VMEM((NP, 2, RX, 128), F32)],
        compiler_params=params(),
        name="leaf_spread",
    )(lists, *crit)


def solve_columns(values, inverse, which, *lead):
    total = None
    for r in range(NX):
        left = jnp.concatenate([values[(8 * r + k, *lead)] for k in range(8)], axis=1)
        term = dot(left, inverse[r, which])
        total = term if total is None else total + term
    return total


def solve_rows(target, inverse, which, store):
    for r in range(NX):
        wide = dot_t(target, inverse[r, which]).astype(BF)
        for k in range(8):
            store(r, k, wide[:, 128 * k : 128 * (k + 1)])


def multiply_update(acc, x, table, pair, local_pair, rounded, factor, *lead):
    for r in range(NX):
        update = dot(rounded, factor[r, local_pair])
        add_update(acc, table, source(x, r), pair, update, *lead)


def pick_product(x, table, pair, local_pair, values, factor, *lead):
    total = None
    for r in range(NX):
        tiles = []
        for j in range(2):
            block = listed(table, source(x, r), pair, j)
            tiles += [values[(2 * block, *lead)], values[(2 * block + 1, *lead)]]
        term = dot_t(jnp.concatenate(tiles, axis=1), factor[r, local_pair])
        total = term if total is None else total + term
    return total


def whole(*shape):
    return pl.BlockSpec(shape, lambda n: (0,) * len(shape))


TILES = whole(NP, RX, 128)
TOP_INVERSE = whole(NX, 1, 1024, 128)
TOP_FACTOR = whole(NX, 1, 128, 512)
VMEM = pl.BlockSpec(memory_space=pltpu.VMEM)


def middle_forward_kernel(x_ref, table, values, inverse, factor, o0, o1, o2, o3, fwd, out, acc_root, acc):
    x = x_ref[0]
    acc[...] = jnp.zeros(acc.shape, F32)
    acc_root[...] = jnp.zeros(acc_root.shape, F32)
    for d, other in enumerate((o0, o1, o2, o3)):
        for n in range(4):
            add_update(acc_root, table, d, 5 + 3 * n, other[2 * n])
            add_update(acc, table, d, 5 + 3 * n + 1, other[2 * n + 1])
    for m in range(2):
        solved = solve_columns(values, inverse, m, m)
        fwd[m] = solved
        rounded = solved.astype(BF)
        multiply_update(acc_root, x, table, 1 + 2 * m, 1 + 2 * m, rounded, factor)
        multiply_update(acc, x, table, 2 + 2 * m, 2 + 2 * m, rounded, factor)
    out[...] = acc[...].astype(BF)


def middle_forward(x, table, values, inverse, factor, other):
    return pl.pallas_call(
        middle_forward_kernel,
        out_shape=[
            jax.ShapeDtypeStruct((2, RX, 128), F32),
            jax.ShapeDtypeStruct((NP, RX, 128), BF),
            jax.ShapeDtypeStruct((NP, RX, 128), F32),
        ],
        in_specs=[SMEM] * 2 + [VMEM] * 7,
        scratch_shapes=[pltpu.VMEM((NP, RX, 128), F32)],
        compiler_params=params(),
        name="middle_forward",
    )(x, table, values, inverse, factor, *other)


def top_forward_kernel(x_ref, table, values, inverse, factor, acc_in, fwd, out, acc):
    acc[...] = acc_in[...]
    solved = solve_columns(values, inverse, 0)
    fwd[...] = solved
    multiply_update(acc, x_ref[0], table, 0, 0, solved.astype(BF), factor)
    out[...] = acc[...].astype(BF)


def top_forward(x, table, values, inverse, factor, acc_root):
    return pl.pallas_call(
        top_forward_kernel,
        grid=(1,),
        out_shape=[
            jax.ShapeDtypeStruct((RX, 128), F32),
            jax.ShapeDtypeStruct((NP, RX, 128), BF),
        ],
        in_specs=[SMEM] * 2 + [TILES, TOP_INVERSE, TOP_FACTOR, TILES],
        out_specs=[whole(RX, 128), TILES],
        scratch_shapes=[pltpu.VMEM((NP, RX, 128), F32)],
        compiler_params=params(),
        name="top_forward",
    )(x, table, values, inverse, factor, acc_root)


def root_kernel(values, inverse, out):
    rounded = solve_columns(values, inverse, 0).astype(BF)

    def store(r, k, tile):
        out[8 * r + k] = tile

    solve_rows(rounded, inverse, 0, store)


def root_solve(values, inverse):
    return pl.pallas_call(
        root_kernel,
        grid=(1,),
        out_shape=jax.ShapeDtypeStruct((NP, RX, 128), BF),
        in_specs=[TILES, pl.BlockSpec((NX, 1, 1024, 128), lambda n: (0, 1, 0, 0))],
        out_specs=TILES,
        compiler_params=params(),
        name="root_solve",
    )(values, inverse)


def top_backward_kernel(x_ref, table, root, fwd, inverse, factor, out):
    down = pick_product(x_ref[0], table, 0, 0, root, factor)

    def store(r, k, tile):
        out[8 * r + k] = tile

    solve_rows((fwd[...] - down).astype(BF), inverse, 0, store)


def top_backward(x, table, root, fwd, inverse, factor):
    return pl.pallas_call(
        top_backward_kernel,
        grid=(1,),
        out_shape=jax.ShapeDtypeStruct((NP, RX, 128), BF),
        in_specs=[SMEM] * 2 + [TILES, whole(RX, 128), TOP_INVERSE, TOP_FACTOR],
        out_specs=TILES,
        compiler_params=params(),
        name="top_backward",
    )(x, table, root, fwd, inverse, factor)


def middle_backward_kernel(x_ref, table, root, top, fwd, inverse, factor, out):
    x = x_ref[0]
    for m in range(2):
        down = pick_product(x, table, 1 + 2 * m, 1 + 2 * m, root, factor)
        down = down + pick_product(x, table, 2 + 2 * m, 2 + 2 * m, top, factor)

        def store(r, k, tile, m=m):
            out[8 * r + k, m] = tile

        solve_rows((fwd[m] - down).astype(BF), inverse, m, store)


def middle_backward(x, table, root, top, fwd, inverse, factor):
    return pl.pallas_call(
        middle_backward_kernel,
        out_shape=jax.ShapeDtypeStruct((NP, 2, RX, 128), BF),
        in_specs=[SMEM] * 2 + [VMEM] * 5,
        compiler_params=params(),
        name="middle_backward",
    )(x, table, root, top, fwd, inverse, factor)


def leaf_backward_kernel(x_ref, table, root, top, middle, fwd, inverse, factor, out):
    x = x_ref[0]
    n = pl.program_id(0)
    first = 5 + 3 * n
    down = pick_product(x, table, first, 0, root, factor)
    down = down + pick_product(x, table, first + 1, 1, top, factor)
    down = down + pick_product(x, table, first + 2, 2, middle, factor, n // 2)

    def store(r, k, tile):
        out[k, r] = tile

    solve_rows((fwd[0] - down).astype(BF), inverse, 0, store)


def leaf_backward(x, table, root, top, middle, fwd, inverse, factor):
    return pl.pallas_call(
        leaf_backward_kernel,
        grid=(4,),
        out_shape=jax.ShapeDtypeStruct((NP, NX, RX, 128), BF),
        in_specs=[SMEM] * 2
        + [TILES, TILES, whole(NP, 2, RX, 128)]
        + [pl.BlockSpec((1, RX, 128), lambda n: (n, 0, 0))]
        + [pl.BlockSpec((NX, 1, 1024, 128), lambda n: (0, n, 0, 0))]
        + [pl.BlockSpec((NX, 3, 128, 512), lambda n: (0, n, 0, 0))],
        out_specs=pl.BlockSpec((8, NX, RX, 128), lambda n: (n, 0, 0, 0)),
        compiler_params=params(),
        name="leaf_backward",
    )(x, table, root, top, middle, fwd, inverse, factor)


def finish_kernel(x_ref, e0, e1, e2, e3, leaves, out_sub, out_root):
    x = x_ref[0]
    for d, early in enumerate((e0, e1, e2, e3)):
        rows = pl.ds(pl.multiple_of(RX * source(x, d), RX), RX)
        for k in range(8):
            columns = slice(128 * k, 128 * (k + 1))
            out_root[rows, columns] = early[k, 0].astype(F32)
            for t in range(3):
                out_sub[t, rows, columns] = early[k, 1 + t].astype(F32)
    for t in range(4):
        for k in range(8):
            out_sub[3 + t, :, 128 * k : 128 * (k + 1)] = leaves[8 * t + k].astype(F32)


def finish(x, early, leaves):
    return pl.pallas_call(
        finish_kernel,
        out_shape=[
            jax.ShapeDtypeStruct((7, 64, 1024), F32),
            jax.ShapeDtypeStruct((64, 1024), F32),
        ],
        in_specs=[SMEM] + [pl.BlockSpec(memory_space=pltpu.VMEM)] * 5,
        compiler_params=params(),
        name="finish",
    )(x, *early, leaves)


def gather_rows(value):
    return lax.all_gather(value, "prow")


def per_device(right_sub, right_root, inverse_sub, inverse_root, factor_blocks, block_lists):
    position = lax.axis_index("prow")
    column = lax.axis_index("pcol")
    x = position.astype(jnp.int32)[None]

    inverse_middle = gather_rows(inverse_sub[1:3])
    factor_upper = gather_rows(factor_blocks[0:5])
    inverse_top = gather_rows(jnp.concatenate([inverse_sub[0:1], inverse_root[None]], 0))
    inverse_leaf = gather_rows(inverse_sub[3:7])
    factor_leaf = gather_rows(factor_blocks[5:17])

    own = jnp.einsum(
        "nrm,nmc->nrc", right_sub[3:7].astype(BF), inverse_sub[3:7], preferred_element_type=F32
    ).astype(BF)
    received = around(own)
    table = jnp.concatenate([value.reshape(-1) for value in around(block_lists)])

    def right_piece(d):
        row = RX * lax.rem(position + d, NX)
        start = 128 * lax.rem(column, 8)
        sub = lax.dynamic_slice(right_sub, (0, row, start), (3, RX, 128))
        root = lax.dynamic_slice(right_root, (row, start), (RX, 128))
        return jnp.concatenate([sub, root[None]], 0)

    right = right_piece(0)
    held = lax.rem(position + NX - column // 8, NX)
    for d in range(1, NX):
        right = jnp.where(held == d, shift(right_piece(d), d), right)

    fwd_leaf, crit, other = leaf_update(x, own, received[1:], factor_blocks[5:17])
    crit = [crit[0]] + [shift(crit[d], d) for d in range(1, NX)]
    other = [other[0]] + [shift(other[d], d) for d in range(1, NX)]

    values = gather_columns(right[1:3] - reduce_columns(leaf_spread(table, crit)))
    fwd_middle, parts, acc_root = middle_forward(
        x, table, values, inverse_middle, factor_upper, other
    )
    values = gather_columns(right[0] - reduce_columns(parts))
    fwd_top, parts = top_forward(x, table, values, inverse_top, factor_upper, acc_root)
    total = reduce_columns(parts)
    total = total + lax.ppermute(total, "layer", [(0, 1), (1, 0)])
    values = gather_columns(right[3] - total)
    root = gather_columns(reduce_columns(root_solve(values, inverse_top)))
    parts = top_backward(x, table, root, fwd_top, inverse_top, factor_upper)
    top = gather_columns(reduce_columns(parts))
    parts = middle_backward(x, table, root, top, fwd_middle, inverse_middle, factor_upper)
    middle = gather_columns(reduce_columns(parts))

    early = jnp.concatenate([root[:, None], top[:, None], middle], 1)
    pieces = []
    for d in range(NX):
        piece = lax.dynamic_slice_in_dim(early, 8 * lax.rem(position + d, NX), 8, 0)
        pieces.append(shift(piece, d) if d else piece)

    parts = leaf_backward(x, table, root, top, middle, fwd_leaf, inverse_leaf, factor_leaf)
    parts = after(parts, *pieces)
    chunk = reduce_columns(parts).astype(BF)
    chunk = lax.all_to_all(chunk, "prow", 0, 0, tiled=True).reshape(4 * RX, 128)
    leaves = gather_columns(chunk)
    return tuple(finish(x, pieces, leaves))


def solution(mesh):
    in_specs = (
        P("layer", None, "prow"),
        P(None, "prow"),
        P("layer", "prow", "pcol"),
        P("prow", "pcol"),
        P("layer", "pcol", "prow"),
        P("layer", "prow"),
    )
    out_specs = (P("layer", None, "prow"), P(None, "prow"))
    return jax.shard_map(
        per_device, mesh=mesh, in_specs=in_specs, out_specs=out_specs, check_vma=False
    )
```

```python
import jax
import jax.numpy as jnp
from jax import lax
from jax.experimental import pallas as pl
from jax.experimental.pallas import tpu as pltpu
from jax.sharding import PartitionSpec as P

NX = 4
NP = 32
RX = 16
BF = jnp.bfloat16
F32 = jnp.float32
LIMIT = 56 * 1024 * 1024

SMEM = pl.BlockSpec(memory_space=pltpu.SMEM)
VMEM = pl.BlockSpec(memory_space=pltpu.VMEM)


def whole(*shape):
    return pl.BlockSpec(shape, lambda n: (0,) * len(shape))


def params():
    return pltpu.CompilerParams(vmem_limit_bytes=LIMIT)


def shift(value, distance):
    return lax.ppermute(value, "prow", [(i, (i + distance) % NX) for i in range(NX)])


def around(value):
    return [value] + [shift(value, distance) for distance in range(1, NX)]


def after(value, *earlier):
    return lax.optimization_barrier((value, *earlier))[0]


def exchange(value):
    return lax.all_to_all(value, "pcol", 0, 0, tiled=True)


def reduce_columns(parts):
    return jnp.sum(exchange(parts).astype(F32), axis=0)


def gather_columns(chunk):
    chunk = chunk.astype(BF)
    return exchange(jnp.broadcast_to(chunk[None], (NP,) + chunk.shape))


def dot(left, right):
    return lax.dot_general(left, right, (((1,), (0,)), ((), ())), preferred_element_type=F32)


def dot_t(left, right):
    return lax.dot_general(left, right, (((1,), (1,)), ((), ())), preferred_element_type=F32)


def row_start(x, distance):
    return pl.multiple_of(lax.rem(x + distance, NX) * RX, RX)


def source(x, distance):
    return lax.rem(x + (NX - distance), NX)


def start_kernel(place, right_sub, right_root, inverse, inverse_root, factor, lists, own, *rest):
    pieces, (middle, top, leaf, rights, inverses, sems) = rest[0:4], rest[4:]
    row, column = place[0], place[1]

    def copy(source_ref, target_ref, index):
        pltpu.make_async_copy(source_ref, target_ref, sems.at[index]).start()

    copy(right_sub.at[3:7], rights, 0)
    copy(inverse.at[3:7], inverses, 1)

    def factor_copy(pair, target, first, index):
        for c in range(4):
            copy(factor.at[pair, :, 128 * c : 128 * (c + 1)], target.at[first + c], index)

    for m in range(2):
        copy(inverse.at[1 + m], middle.at[m, 0:8], 2)
        for i in range(2):
            factor_copy(1 + 2 * m + i, middle.at[m], 8 + 4 * i, 2)
    for d in range(NX):
        rows = pl.ds(row_start(row, d), RX)
        columns = pl.ds(pl.multiple_of(128 * column, 128), 128)
        copy(right_sub.at[0:3, rows, columns], pieces[d].at[0:3], 5 + d)
        copy(right_root.at[rows, columns], pieces[d].at[3], 5 + d)
        copy(lists, pieces[d].at[4], 5 + d)
    copy(inverse_root, top.at[0:8], 3)
    copy(inverse.at[0], top.at[8:16], 3)
    factor_copy(0, top, 16, 3)

    def leaf_copies(n, carry):
        copy(inverse.at[3 + n], leaf.at[n, 0:8], 4)
        for i in range(3):
            factor_copy(5 + 3 * n + i, leaf.at[n], (12, 16, 8)[i], 4)
        return carry

    lax.fori_loop(0, 4, leaf_copies, 0)
    pltpu.make_async_copy(rights, rights, sems.at[0]).wait()
    pltpu.make_async_copy(inverses, inverses, sems.at[1]).wait()
    for n in range(4):
        own[n] = dot(rights[n].astype(BF), inverses[n].reshape(1024, 128)).astype(BF)
    for target, index in ((middle, 2), (top, 3), (leaf, 4)):
        pltpu.make_async_copy(target, target, sems.at[index]).wait()
    for d in range(NX):
        pltpu.make_async_copy(pieces[d], pieces[d], sems.at[5 + d]).wait()


def start(place, right_sub, right_root, inverse, inverse_root, factor, lists):
    hbm = pl.BlockSpec(memory_space=pl.ANY)
    result = pl.pallas_call(
        start_kernel,
        out_shape=[jax.ShapeDtypeStruct((4, 64, 128), BF)]
        + [jax.ShapeDtypeStruct((5, RX, 128), F32)] * 4
        + [
            jax.ShapeDtypeStruct((2, 16, 128, 128), BF),
            jax.ShapeDtypeStruct((20, 128, 128), BF),
            jax.ShapeDtypeStruct((4, 20, 128, 128), BF),
        ],
        in_specs=[SMEM] + [hbm] * 6,
        out_specs=[VMEM] * 8,
        scratch_shapes=[
            pltpu.VMEM((4, 64, 1024), F32),
            pltpu.VMEM((4, 8, 128, 128), BF),
            pltpu.SemaphoreType.DMA((9,)),
        ],
        compiler_params=params(),
        name="start",
    )(
        place,
        right_sub,
        right_root,
        inverse.reshape(7, 8, 128, 128),
        inverse_root.reshape(8, 128, 128),
        factor,
        lists,
    )
    return result[0], result[1:5], result[5], result[6], result[7]


def leaf_update_kernel(x_ref, own, r1, r2, r3, f0, f1, f2, fwd, *rest):
    crit, other = rest[0:4], rest[4:8]
    x, n = x_ref[0], pl.program_id(0)

    def total(d):
        rows = pl.ds(row_start(x, d), RX)
        parts = [part[n, rows, :].astype(F32) for part in (own, r1, r2, r3)]
        return (parts[0] + parts[1]) + (parts[2] + parts[3])

    solved = [total(d) for d in range(NX)]
    fwd[n] = solved[0]
    left = jnp.concatenate(solved, axis=0).astype(BF)
    for i, factor in enumerate((f0, f1, f2)):
        update = dot(left, factor[0]).astype(BF)
        for d in range(NX):
            piece = update[RX * d : RX * (d + 1)]
            if i == 2:
                crit[d][n] = piece
            else:
                other[d][2 * n + i] = piece


def leaf_update(x, own, received, factor):
    part = whole(4, 64, 128)
    result = pl.pallas_call(
        leaf_update_kernel,
        grid=(4,),
        out_shape=[jax.ShapeDtypeStruct((4, RX, 128), F32)]
        + [jax.ShapeDtypeStruct((4, RX, 512), BF)] * 4
        + [jax.ShapeDtypeStruct((8, RX, 512), BF)] * 4,
        in_specs=[SMEM]
        + [part] * 4
        + [pl.BlockSpec((1, 128, 512), lambda n, i=i: (5 + 3 * n + i, 0, 0)) for i in range(3)],
        out_specs=[whole(4, RX, 128)] + [whole(4, RX, 512)] * 4 + [whole(8, RX, 512)] * 4,
        compiler_params=params(),
        name="leaf_update",
    )(x, own, *received, factor, factor, factor)
    return result[0], result[1:5], result[5:9]


def listed(table, distance, pair, j):
    return table[(distance * 17 + pair) * 2 + j]


def add_update(acc, table, distance, pair, update, *lead):
    for j in range(2):
        block = listed(table, distance, pair, j)
        for h in range(2):
            index = (2 * block + h, *lead)
            tile = update[:, 256 * j + 128 * h : 256 * j + 128 * (h + 1)]
            acc[index] = acc[index] + tile.astype(F32)


def leaf_spread_kernel(lists, c0, c1, c2, c3, out, acc):
    acc[...] = jnp.zeros(acc.shape, F32)
    for d, crit in enumerate((c0, c1, c2, c3)):
        for n in range(4):
            add_update(acc, lists, d, 5 + 3 * n + 2, crit[n], n // 2)
    out[...] = acc[...].astype(BF)


def leaf_spread(lists, crit):
    return pl.pallas_call(
        leaf_spread_kernel,
        out_shape=jax.ShapeDtypeStruct((NP, 2, RX, 128), BF),
        in_specs=[SMEM] + [pl.BlockSpec(memory_space=pltpu.VMEM)] * 4,
        scratch_shapes=[pltpu.VMEM((NP, 2, RX, 128), F32)],
        compiler_params=params(),
        name="leaf_spread",
    )(lists, *crit)


def inverse_share(tiles):
    return tiles.reshape(1024, 128)


def factor_share(tiles):
    return jnp.concatenate([tiles[c] for c in range(4)], axis=1)


def solve_columns(values, inverse, *lead):
    total = None
    for r in range(NX):
        left = jnp.concatenate([values[(8 * r + k, *lead)] for k in range(8)], axis=1)
        term = dot(left, inverse(r))
        total = term if total is None else total + term
    return total


def solve_rows(target, inverse, store):
    for r in range(NX):
        wide = dot_t(target, inverse(r)).astype(BF)
        for k in range(8):
            store(r, k, wide[:, 128 * k : 128 * (k + 1)])


def multiply_update(acc, x, table, pair, rounded, factor, *lead):
    for r in range(NX):
        update = dot(rounded, factor(r))
        add_update(acc, table, source(x, r), pair, update, *lead)


def pick_product(x, table, pair, values, factor, *lead):
    total = None
    for r in range(NX):
        tiles = []
        for j in range(2):
            block = listed(table, source(x, r), pair, j)
            tiles += [values[(2 * block, *lead)], values[(2 * block + 1, *lead)]]
        term = dot_t(jnp.concatenate(tiles, axis=1), factor(r))
        total = term if total is None else total + term
    return total


TILES = whole(NP, RX, 128)
TOP_INVERSE = pl.BlockSpec((NX, 8, 128, 128), lambda n: (0, 1, 0, 0))
TOP_FACTOR = pl.BlockSpec((NX, 4, 128, 128), lambda n: (0, 4, 0, 0))


def middle_inverse(weights, m):
    return lambda r: inverse_share(weights[r, m, 0:8])


def middle_factor(weights, m, i):
    return lambda r: factor_share(weights[r, m, 8 + 4 * i : 12 + 4 * i])


def middle_forward_kernel(x_ref, table, values, weights, o0, o1, o2, o3, fwd, out, acc_root, acc):
    x = x_ref[0]
    acc[...] = jnp.zeros(acc.shape, F32)
    acc_root[...] = jnp.zeros(acc_root.shape, F32)
    for d, other in enumerate((o0, o1, o2, o3)):
        for n in range(4):
            add_update(acc_root, table, d, 5 + 3 * n, other[2 * n])
            add_update(acc, table, d, 5 + 3 * n + 1, other[2 * n + 1])
    for m in range(2):
        solved = solve_columns(values, middle_inverse(weights, m), m)
        fwd[m] = solved
        rounded = solved.astype(BF)
        multiply_update(acc_root, x, table, 1 + 2 * m, rounded, middle_factor(weights, m, 0))
        multiply_update(acc, x, table, 2 + 2 * m, rounded, middle_factor(weights, m, 1))
    out[...] = acc[...].astype(BF)


def middle_forward(x, table, values, weights, other):
    return pl.pallas_call(
        middle_forward_kernel,
        out_shape=[
            jax.ShapeDtypeStruct((2, RX, 128), F32),
            jax.ShapeDtypeStruct((NP, RX, 128), BF),
            jax.ShapeDtypeStruct((NP, RX, 128), F32),
        ],
        in_specs=[SMEM] * 2 + [VMEM] * 6,
        scratch_shapes=[pltpu.VMEM((NP, RX, 128), F32)],
        compiler_params=params(),
        name="middle_forward",
    )(x, table, values, weights, *other)


def top_forward_kernel(x_ref, table, values, inverse, factor, acc_in, fwd, out, acc):
    acc[...] = acc_in[...]
    solved = solve_columns(values, lambda r: inverse_share(inverse[r]))
    fwd[...] = solved
    multiply_update(
        acc, x_ref[0], table, 0, solved.astype(BF), lambda r: factor_share(factor[r])
    )
    out[...] = acc[...].astype(BF)


def top_forward(x, table, values, weights, acc_root):
    return pl.pallas_call(
        top_forward_kernel,
        grid=(1,),
        out_shape=[
            jax.ShapeDtypeStruct((RX, 128), F32),
            jax.ShapeDtypeStruct((NP, RX, 128), BF),
        ],
        in_specs=[SMEM] * 2 + [TILES, TOP_INVERSE, TOP_FACTOR, TILES],
        out_specs=[whole(RX, 128), TILES],
        scratch_shapes=[pltpu.VMEM((NP, RX, 128), F32)],
        compiler_params=params(),
        name="top_forward",
    )(x, table, values, weights, weights, acc_root)


def root_kernel(values, weights, out):
    inverse = lambda r: inverse_share(weights[r])
    rounded = solve_columns(values, inverse).astype(BF)

    def store(r, k, tile):
        out[8 * r + k] = tile

    solve_rows(rounded, inverse, store)


def root_solve(values, weights):
    return pl.pallas_call(
        root_kernel,
        grid=(1,),
        out_shape=jax.ShapeDtypeStruct((NP, RX, 128), BF),
        in_specs=[TILES, whole(NX, 8, 128, 128)],
        out_specs=TILES,
        compiler_params=params(),
        name="root_solve",
    )(values, weights)


def top_backward_kernel(x_ref, table, root, fwd, inverse, factor, out):
    down = pick_product(x_ref[0], table, 0, root, lambda r: factor_share(factor[r]))

    def store(r, k, tile):
        out[8 * r + k] = tile

    solve_rows((fwd[...] - down).astype(BF), lambda r: inverse_share(inverse[r]), store)


def top_backward(x, table, root, fwd, weights):
    return pl.pallas_call(
        top_backward_kernel,
        grid=(1,),
        out_shape=jax.ShapeDtypeStruct((NP, RX, 128), BF),
        in_specs=[SMEM] * 2 + [TILES, whole(RX, 128), TOP_INVERSE, TOP_FACTOR],
        out_specs=TILES,
        compiler_params=params(),
        name="top_backward",
    )(x, table, root, fwd, weights, weights)


def middle_backward_kernel(x_ref, table, root, top, fwd, weights, out):
    x = x_ref[0]
    for m in range(2):
        down = pick_product(x, table, 1 + 2 * m, root, middle_factor(weights, m, 0))
        down = down + pick_product(x, table, 2 + 2 * m, top, middle_factor(weights, m, 1))

        def store(r, k, tile, m=m):
            out[8 * r + k, m] = tile

        solve_rows((fwd[m] - down).astype(BF), middle_inverse(weights, m), store)


def middle_backward(x, table, root, top, fwd, weights):
    return pl.pallas_call(
        middle_backward_kernel,
        out_shape=jax.ShapeDtypeStruct((NP, 2, RX, 128), BF),
        in_specs=[SMEM] * 2 + [VMEM] * 4,
        compiler_params=params(),
        name="middle_backward",
    )(x, table, root, top, fwd, weights)


def leaf_down_kernel(x_ref, table, root, top, fwd, to_root, to_top, out):
    x = x_ref[0]
    first = 5 + 3 * pl.program_id(0)
    down = pick_product(x, table, first, root, lambda r: factor_share(to_root[r, 0]))
    down = down + pick_product(x, table, first + 1, top, lambda r: factor_share(to_top[r, 0]))
    out[0] = fwd[0] - down


def leaf_down(x, table, root, top, fwd, weights):
    factor_at = lambda i: pl.BlockSpec((NX, 1, 4, 128, 128), lambda n: (0, n, i, 0, 0))
    return pl.pallas_call(
        leaf_down_kernel,
        grid=(4,),
        out_shape=jax.ShapeDtypeStruct((4, RX, 128), F32),
        in_specs=[SMEM] * 2
        + [TILES, TILES, pl.BlockSpec((1, RX, 128), lambda n: (n, 0, 0)), factor_at(3), factor_at(4)],
        out_specs=pl.BlockSpec((1, RX, 128), lambda n: (n, 0, 0)),
        compiler_params=params(),
        name="leaf_down",
    )(x, table, root, top, fwd, weights, weights)


def leaf_backward_kernel(x_ref, table, middle, fwd, weights, out):
    x, n = x_ref[0], pl.program_id(0)
    down = pick_product(
        x, table, 7 + 3 * n, middle, lambda r: factor_share(weights[r, 0, 8:12]), n // 2
    )

    def store(r, k, tile):
        out[k, lax.rem(r + NX - x, NX)] = tile

    inverse = lambda r: inverse_share(weights[r, 0, 0:8])
    solve_rows((fwd[0] - down).astype(BF), inverse, store)


def leaf_backward(x, table, middle, fwd, weights):
    return pl.pallas_call(
        leaf_backward_kernel,
        grid=(4,),
        out_shape=jax.ShapeDtypeStruct((NP, NX, RX, 128), BF),
        in_specs=[SMEM] * 2
        + [
            whole(NP, 2, RX, 128),
            pl.BlockSpec((1, RX, 128), lambda n: (n, 0, 0)),
            pl.BlockSpec((NX, 1, 12, 128, 128), lambda n: (0, n, 0, 0, 0)),
        ],
        out_specs=pl.BlockSpec((8, NX, RX, 128), lambda n: (n, 0, 0, 0)),
        compiler_params=params(),
        name="leaf_backward",
    )(x, table, middle, fwd, weights)


def finish_kernel(x_ref, e0, e1, e2, e3, leaves, out_sub, out_root):
    x = x_ref[0]
    for d, early in enumerate((e0, e1, e2, e3)):
        rows = pl.ds(pl.multiple_of(RX * source(x, d), RX), RX)
        for k in range(8):
            columns = slice(128 * k, 128 * (k + 1))
            out_root[rows, columns] = early[k, 0].astype(F32)
            for t in range(3):
                out_sub[t, rows, columns] = early[k, 1 + t].astype(F32)
            for t in range(4):
                out_sub[3 + t, rows, columns] = leaves[8 * t + k, d].astype(F32)


def finish(x, early, leaves):
    return pl.pallas_call(
        finish_kernel,
        out_shape=[
            jax.ShapeDtypeStruct((7, 64, 1024), F32),
            jax.ShapeDtypeStruct((64, 1024), F32),
        ],
        in_specs=[SMEM] + [pl.BlockSpec(memory_space=pltpu.VMEM)] * 5,
        compiler_params=params(),
        name="finish",
    )(x, *early, leaves)


def gather_rows(value):
    return lax.all_gather(value, "prow")


def per_device(right_sub, right_root, inverse_sub, inverse_root, factor_blocks, block_lists):
    position = lax.axis_index("prow").astype(jnp.int32)
    column = lax.axis_index("pcol").astype(jnp.int32)
    x = position[None]
    lists = jnp.pad(block_lists.astype(F32).reshape(1, 34), ((0, RX - 1), (0, 94)))
    own, pieces, middle_weights, top_weights, leaf_weights = start(
        jnp.stack([position, column % 8]),
        right_sub,
        right_root,
        inverse_sub,
        inverse_root,
        factor_blocks,
        lists,
    )
    middle_weights = gather_rows(middle_weights)
    top_weights = gather_rows(top_weights)
    leaf_weights = gather_rows(leaf_weights)

    received = around(own)
    pieces = [pieces[0]] + [shift(pieces[d], d) for d in range(1, NX)]
    table = jnp.concatenate([piece[4, 0, :34] for piece in pieces]).astype(jnp.int32)
    held = lax.rem(position + NX - column // 8, NX)
    right = pieces[0][:4]
    for d in range(1, NX):
        right = jnp.where(held == d, pieces[d][:4], right)

    fwd_leaf, crit, other = leaf_update(x, own, received[1:], factor_blocks)
    crit = [crit[0]] + [shift(crit[d], d) for d in range(1, NX)]
    other = [other[0]] + [shift(other[d], d) for d in range(1, NX)]
    crit[0], right = lax.optimization_barrier((crit[0], right))
    parts = leaf_spread(table, crit)

    values = gather_columns(right[1:3] - reduce_columns(parts))
    fwd_middle, parts, acc_root = middle_forward(x, table, values, middle_weights, other)
    values = gather_columns(right[0] - reduce_columns(parts))
    fwd_top, parts = top_forward(x, table, values, top_weights, acc_root)
    total = reduce_columns(parts)
    total = total + lax.ppermute(total, "layer", [(0, 1), (1, 0)])
    values = gather_columns(right[3] - total)
    root = gather_columns(reduce_columns(root_solve(values, top_weights)))
    parts = top_backward(x, table, root, fwd_top, top_weights)
    top = gather_columns(reduce_columns(parts))
    parts = middle_backward(x, table, root, top, fwd_middle, middle_weights)
    fwd_leaf = leaf_down(x, table, root, top, fwd_leaf, leaf_weights)
    middle = gather_columns(reduce_columns(parts))

    early = jnp.concatenate([root[:, None], top[:, None], middle], 1)
    pieces = []
    for d in range(NX):
        piece = lax.dynamic_slice_in_dim(early, 8 * lax.rem(position + d, NX), 8, 0)
        pieces.append(shift(piece, d) if d else piece)

    parts = leaf_backward(x, table, middle, fwd_leaf, leaf_weights)
    chunk = reduce_columns(parts).astype(BF)
    chunk = jnp.stack([chunk[0]] + [shift(chunk[d], d) for d in range(1, NX)])
    leaves = gather_columns(after(chunk, *pieces))
    return tuple(finish(x, pieces, leaves))


def solution(mesh):
    in_specs = (
        P("layer", None, "prow"),
        P(None, "prow"),
        P("layer", "prow", "pcol"),
        P("prow", "pcol"),
        P("layer", "pcol", "prow"),
        P("layer", "prow"),
    )
    out_specs = (P("layer", None, "prow"), P(None, "prow"))
    return jax.shard_map(
        per_device, mesh=mesh, in_specs=in_specs, out_specs=out_specs, check_vma=False
    )
```

```python
import jax
import jax.numpy as jnp
from jax import lax
from jax.experimental import pallas as pl
from jax.experimental.pallas import tpu as pltpu
from jax.sharding import PartitionSpec as P

NX = 4
NP = 32
RX = 16
BF = jnp.bfloat16
F32 = jnp.float32
LIMIT = 14 * 1024 * 1024
LARGE = 56 * 1024 * 1024

SMEM = pl.BlockSpec(memory_space=pltpu.SMEM)
VMEM = pl.BlockSpec(memory_space=pltpu.VMEM)


def whole(*shape):
    return pl.BlockSpec(shape, lambda n: (0,) * len(shape))


def params(limit=LIMIT):
    return pltpu.CompilerParams(vmem_limit_bytes=limit)


def shift(value, distance):
    return lax.ppermute(value, "prow", [(i, (i + distance) % NX) for i in range(NX)])


def around(value):
    return [value] + [shift(value, distance) for distance in range(1, NX)]


def after(value, *earlier):
    return lax.optimization_barrier((value, *earlier))[0]


def exchange(value):
    return lax.all_to_all(value, "pcol", 0, 0, tiled=True)


def reduce_columns(parts):
    return jnp.sum(exchange(parts).astype(F32), axis=0)


def gather_columns(chunk):
    chunk = chunk.astype(BF)
    return exchange(jnp.broadcast_to(chunk[None], (NP,) + chunk.shape))


def dot(left, right):
    return lax.dot_general(left, right, (((1,), (0,)), ((), ())), preferred_element_type=F32)


def dot_t(left, right):
    return lax.dot_general(left, right, (((1,), (1,)), ((), ())), preferred_element_type=F32)


def row_start(x, distance):
    return pl.multiple_of(lax.rem(x + distance, NX) * RX, RX)


def source(x, distance):
    return lax.rem(x + (NX - distance), NX)


SENT = 25


def start_kernel(place, right_sub, right_root, inverse, inverse_root, factor, lists, sent, middle, top, rights, inverses, pieces, sems):
    column = place[0]

    def copy(source_ref, target_ref, index):
        pltpu.make_async_copy(source_ref, target_ref, sems.at[index]).start()

    copy(right_sub.at[3:7], rights, 0)
    copy(inverse.at[3:7], inverses, 1)
    columns = pl.ds(pl.multiple_of(128 * column, 128), 128)
    copy(right_sub.at[0:3, :, columns], pieces.at[0:3], 4)
    copy(right_root.at[:, columns], pieces.at[3], 4)

    def factor_copy(pair, target, first, index):
        for c in range(4):
            copy(factor.at[pair, :, 128 * c : 128 * (c + 1)], target.at[first + c], index)

    for m in range(2):
        copy(inverse.at[1 + m], middle.at[m, 0:8], 2)
        for i in range(2):
            factor_copy(1 + 2 * m + i, middle.at[m], 8 + 4 * i, 2)
    copy(inverse_root, top.at[0:8], 3)
    copy(inverse.at[0], top.at[8:16], 3)
    factor_copy(0, top, 16, 3)

    names = lists[...].astype(F32).astype(BF)
    pltpu.make_async_copy(pieces, pieces, sems.at[4]).wait()
    for r in range(NX):
        sent[r, 24] = jnp.zeros((RX, 128), BF)
        sent[r, 24, 0:2, 0:17] = names
        for t in range(4):
            piece = pieces[t, RX * r : RX * (r + 1), :]
            high = piece.astype(BF)
            sent[r, 16 + t] = high
            sent[r, 20 + t] = (piece - high.astype(F32)).astype(BF)
    pltpu.make_async_copy(rights, rights, sems.at[0]).wait()
    pltpu.make_async_copy(inverses, inverses, sems.at[1]).wait()
    for n in range(4):
        own = dot(rights[n].astype(BF), inverses[n].reshape(1024, 128)).astype(BF)
        for r in range(NX):
            for g in range(NX):
                sent[r, 4 * n + g] = own[RX * g : RX * (g + 1)]
    pltpu.make_async_copy(middle, middle, sems.at[2]).wait()
    pltpu.make_async_copy(top, top, sems.at[3]).wait()


def start(place, right_sub, right_root, inverse, inverse_root, factor, lists):
    hbm = pl.BlockSpec(memory_space=pl.ANY)
    return pl.pallas_call(
        start_kernel,
        out_shape=[
            jax.ShapeDtypeStruct((NX, SENT, RX, 128), BF),
            jax.ShapeDtypeStruct((2, 16, 128, 128), BF),
            jax.ShapeDtypeStruct((20, 128, 128), BF),
        ],
        in_specs=[SMEM] + [hbm] * 5 + [VMEM],
        out_specs=[VMEM] * 3,
        scratch_shapes=[
            pltpu.VMEM((4, 64, 1024), F32),
            pltpu.VMEM((4, 8, 128, 128), BF),
            pltpu.VMEM((4, 64, 128), F32),
            pltpu.SemaphoreType.DMA((5,)),
        ],
        compiler_params=params(LARGE),
        name="start",
    )(place, right_sub, right_root, inverse, inverse_root, factor, lists)


def leaf_update_kernel(x_ref, got, inverse, f0, f1, f2, fwd, *rest):
    crit, other, packed = rest[0:4], rest[4:8], rest[8]
    x, n = x_ref[0], pl.program_id(0)

    def total(d):
        tile = 4 * n + lax.rem(x + d, NX)
        parts = [got[r, tile].astype(F32) for r in range(NX)]
        return (parts[0] + parts[1]) + (parts[2] + parts[3])

    solved = [total(d) for d in range(NX)]
    fwd[n] = solved[0]
    left = jnp.concatenate(solved, axis=0).astype(BF)
    packed[0, 0:8] = inverse[0]
    for i, factor in enumerate((f0, f1, f2)):
        first = (12, 16, 8)[i]
        for c in range(4):
            packed[0, first + c] = factor[0, :, 128 * c : 128 * (c + 1)]
        update = dot(left, factor[0]).astype(BF)
        for d in range(NX):
            piece = update[RX * d : RX * (d + 1)]
            if i == 2:
                crit[d][n] = piece
            else:
                other[d][2 * n + i] = piece


def leaf_update(x, got, inverse, factor):
    result = pl.pallas_call(
        leaf_update_kernel,
        grid=(4,),
        out_shape=[jax.ShapeDtypeStruct((4, RX, 128), F32)]
        + [jax.ShapeDtypeStruct((4, RX, 512), BF)] * 4
        + [jax.ShapeDtypeStruct((8, RX, 512), BF)] * 4
        + [jax.ShapeDtypeStruct((4, 20, 128, 128), BF)],
        in_specs=[
            SMEM,
            whole(NX, SENT, RX, 128),
            pl.BlockSpec((1, 8, 128, 128), lambda n: (3 + n, 0, 0, 0)),
        ]
        + [pl.BlockSpec((1, 128, 512), lambda n, i=i: (5 + 3 * n + i, 0, 0)) for i in range(3)],
        out_specs=[whole(4, RX, 128)]
        + [whole(4, RX, 512)] * 4
        + [whole(8, RX, 512)] * 4
        + [pl.BlockSpec((1, 20, 128, 128), lambda n: (n, 0, 0, 0))],
        compiler_params=params(LARGE),
        name="leaf_update",
    )(x, got, inverse, factor, factor, factor)
    return result[0], result[1:5], result[5:9], result[9]


def listed(table, r, pair, j):
    return table[r, j, pair]


def add_update(acc, table, r, pair, update, *lead):
    for j in range(2):
        block = listed(table, r, pair, j)
        for h in range(2):
            index = (2 * block + h, *lead)
            tile = update[:, 256 * j + 128 * h : 256 * j + 128 * (h + 1)]
            acc[index] = acc[index] + tile.astype(F32)


def leaf_spread_kernel(x_ref, table, c0, c1, c2, c3, out, acc):
    x = x_ref[0]
    acc[...] = jnp.zeros(acc.shape, F32)
    for d, crit in enumerate((c0, c1, c2, c3)):
        for n in range(4):
            add_update(acc, table, source(x, d), 5 + 3 * n + 2, crit[n], n // 2)
    out[...] = acc[...].astype(BF)


def leaf_spread(x, table, crit):
    return pl.pallas_call(
        leaf_spread_kernel,
        out_shape=jax.ShapeDtypeStruct((NP, 2, RX, 128), BF),
        in_specs=[SMEM] * 2 + [VMEM] * 4,
        scratch_shapes=[pltpu.VMEM((NP, 2, RX, 128), F32)],
        compiler_params=params(),
        name="leaf_spread",
    )(x, table, *crit)


def inverse_share(tiles):
    return tiles.reshape(1024, 128)


def factor_share(tiles):
    return jnp.concatenate([tiles[c] for c in range(4)], axis=1)


def solve_columns(values, inverse, *lead):
    total = None
    for r in range(NX):
        left = jnp.concatenate([values[(8 * r + k, *lead)] for k in range(8)], axis=1)
        term = dot(left, inverse(r))
        total = term if total is None else total + term
    return total


def solve_rows(target, inverse, store):
    for r in range(NX):
        wide = dot_t(target, inverse(r)).astype(BF)
        for k in range(8):
            store(r, k, wide[:, 128 * k : 128 * (k + 1)])


def multiply_update(acc, x, table, pair, rounded, factor, *lead):
    for r in range(NX):
        update = dot(rounded, factor(r))
        add_update(acc, table, r, pair, update, *lead)


def pick_product(x, table, pair, values, factor, *lead):
    total = None
    for r in range(NX):
        tiles = []
        for j in range(2):
            block = listed(table, r, pair, j)
            tiles += [values[(2 * block, *lead)], values[(2 * block + 1, *lead)]]
        term = dot_t(jnp.concatenate(tiles, axis=1), factor(r))
        total = term if total is None else total + term
    return total


TILES = whole(NP, RX, 128)
TOP_INVERSE = pl.BlockSpec((NX, 8, 128, 128), lambda n: (0, 1, 0, 0))
TOP_FACTOR = pl.BlockSpec((NX, 4, 128, 128), lambda n: (0, 4, 0, 0))


def middle_inverse(weights, m):
    return lambda r: inverse_share(weights[r, m, 0:8])


def middle_factor(weights, m, i):
    return lambda r: factor_share(weights[r, m, 8 + 4 * i : 12 + 4 * i])


def middle_forward_kernel(x_ref, table, values, weights, o0, o1, o2, o3, fwd, out, acc_root, acc):
    x = x_ref[0]
    acc[...] = jnp.zeros(acc.shape, F32)
    acc_root[...] = jnp.zeros(acc_root.shape, F32)
    for d, other in enumerate((o0, o1, o2, o3)):
        for n in range(4):
            r = source(x, d)
            add_update(acc_root, table, r, 5 + 3 * n, other[2 * n])
            add_update(acc, table, r, 5 + 3 * n + 1, other[2 * n + 1])
    for m in range(2):
        solved = solve_columns(values, middle_inverse(weights, m), m)
        fwd[m] = solved
        rounded = solved.astype(BF)
        multiply_update(acc_root, x, table, 1 + 2 * m, rounded, middle_factor(weights, m, 0))
        multiply_update(acc, x, table, 2 + 2 * m, rounded, middle_factor(weights, m, 1))
    out[...] = acc[...].astype(BF)


def middle_forward(x, table, values, weights, other):
    return pl.pallas_call(
        middle_forward_kernel,
        out_shape=[
            jax.ShapeDtypeStruct((2, RX, 128), F32),
            jax.ShapeDtypeStruct((NP, RX, 128), BF),
            jax.ShapeDtypeStruct((NP, RX, 128), F32),
        ],
        in_specs=[SMEM] * 2 + [VMEM] * 6,
        scratch_shapes=[pltpu.VMEM((NP, RX, 128), F32)],
        compiler_params=params(),
        name="middle_forward",
    )(x, table, values, weights, *other)


def top_forward_kernel(x_ref, table, values, inverse, factor, acc_in, fwd, out, acc):
    acc[...] = acc_in[...]
    solved = solve_columns(values, lambda r: inverse_share(inverse[r]))
    fwd[...] = solved
    multiply_update(
        acc, x_ref[0], table, 0, solved.astype(BF), lambda r: factor_share(factor[r])
    )
    out[...] = acc[...].astype(BF)


def top_forward(x, table, values, weights, acc_root):
    return pl.pallas_call(
        top_forward_kernel,
        grid=(1,),
        out_shape=[
            jax.ShapeDtypeStruct((RX, 128), F32),
            jax.ShapeDtypeStruct((NP, RX, 128), BF),
        ],
        in_specs=[SMEM] * 2 + [TILES, TOP_INVERSE, TOP_FACTOR, TILES],
        out_specs=[whole(RX, 128), TILES],
        scratch_shapes=[pltpu.VMEM((NP, RX, 128), F32)],
        compiler_params=params(),
        name="top_forward",
    )(x, table, values, weights, weights, acc_root)


def root_kernel(values, weights, out):
    inverse = lambda r: inverse_share(weights[r])
    rounded = solve_columns(values, inverse).astype(BF)

    def store(r, k, tile):
        out[8 * r + k] = tile

    solve_rows(rounded, inverse, store)


def root_solve(values, weights):
    return pl.pallas_call(
        root_kernel,
        grid=(1,),
        out_shape=jax.ShapeDtypeStruct((NP, RX, 128), BF),
        in_specs=[TILES, whole(NX, 8, 128, 128)],
        out_specs=TILES,
        compiler_params=params(),
        name="root_solve",
    )(values, weights)


def top_backward_kernel(x_ref, table, root, fwd, inverse, factor, out):
    down = pick_product(x_ref[0], table, 0, root, lambda r: factor_share(factor[r]))

    def store(r, k, tile):
        out[8 * r + k] = tile

    solve_rows((fwd[...] - down).astype(BF), lambda r: inverse_share(inverse[r]), store)


def top_backward(x, table, root, fwd, weights):
    return pl.pallas_call(
        top_backward_kernel,
        grid=(1,),
        out_shape=jax.ShapeDtypeStruct((NP, RX, 128), BF),
        in_specs=[SMEM] * 2 + [TILES, whole(RX, 128), TOP_INVERSE, TOP_FACTOR],
        out_specs=TILES,
        compiler_params=params(),
        name="top_backward",
    )(x, table, root, fwd, weights, weights)


def middle_backward_kernel(x_ref, table, root, top, fwd, weights, out):
    x = x_ref[0]
    for m in range(2):
        down = pick_product(x, table, 1 + 2 * m, root, middle_factor(weights, m, 0))
        down = down + pick_product(x, table, 2 + 2 * m, top, middle_factor(weights, m, 1))

        def store(r, k, tile, m=m):
            out[8 * r + k, m] = tile

        solve_rows((fwd[m] - down).astype(BF), middle_inverse(weights, m), store)


def middle_backward(x, table, root, top, fwd, weights):
    return pl.pallas_call(
        middle_backward_kernel,
        out_shape=jax.ShapeDtypeStruct((NP, 2, RX, 128), BF),
        in_specs=[SMEM] * 2 + [VMEM] * 4,
        compiler_params=params(LARGE),
        name="middle_backward",
    )(x, table, root, top, fwd, weights)


def leaf_down_kernel(x_ref, table, root, top, fwd, to_root, to_top, out):
    x = x_ref[0]
    first = 5 + 3 * pl.program_id(0)
    down = pick_product(x, table, first, root, lambda r: factor_share(to_root[r, 0]))
    down = down + pick_product(x, table, first + 1, top, lambda r: factor_share(to_top[r, 0]))
    out[0] = fwd[0] - down


def leaf_down(x, table, root, top, fwd, weights):
    factor_at = lambda i: pl.BlockSpec((NX, 1, 4, 128, 128), lambda n: (0, n, i, 0, 0))
    return pl.pallas_call(
        leaf_down_kernel,
        grid=(4,),
        out_shape=jax.ShapeDtypeStruct((4, RX, 128), F32),
        in_specs=[SMEM] * 2
        + [TILES, TILES, pl.BlockSpec((1, RX, 128), lambda n: (n, 0, 0)), factor_at(3), factor_at(4)],
        out_specs=pl.BlockSpec((1, RX, 128), lambda n: (n, 0, 0)),
        compiler_params=params(LARGE),
        name="leaf_down",
    )(x, table, root, top, fwd, weights, weights)


def leaf_backward_kernel(x_ref, table, middle, fwd, weights, out):
    x, n = x_ref[0], pl.program_id(0)
    down = pick_product(
        x, table, 7 + 3 * n, middle, lambda r: factor_share(weights[r, 0, 8:12]), n // 2
    )

    def store(r, k, tile):
        out[k, lax.rem(r + NX - x, NX)] = tile

    inverse = lambda r: inverse_share(weights[r, 0, 0:8])
    solve_rows((fwd[0] - down).astype(BF), inverse, store)


def leaf_backward(x, table, middle, fwd, weights):
    return pl.pallas_call(
        leaf_backward_kernel,
        grid=(4,),
        out_shape=jax.ShapeDtypeStruct((NP, NX, RX, 128), BF),
        in_specs=[SMEM] * 2
        + [
            whole(NP, 2, RX, 128),
            pl.BlockSpec((1, RX, 128), lambda n: (n, 0, 0)),
            pl.BlockSpec((NX, 1, 12, 128, 128), lambda n: (0, n, 0, 0, 0)),
        ],
        out_specs=pl.BlockSpec((8, NX, RX, 128), lambda n: (n, 0, 0, 0)),
        compiler_params=params(LARGE),
        name="leaf_backward",
    )(x, table, middle, fwd, weights)


def finish_kernel(x_ref, e0, e1, e2, e3, leaves, out_sub, out_root):
    x = x_ref[0]
    for d, early in enumerate((e0, e1, e2, e3)):
        rows = pl.ds(pl.multiple_of(RX * source(x, d), RX), RX)
        for k in range(8):
            columns = slice(128 * k, 128 * (k + 1))
            out_root[rows, columns] = early[k, 0].astype(F32)
            for t in range(3):
                out_sub[t, rows, columns] = early[k, 1 + t].astype(F32)
            for t in range(4):
                out_sub[3 + t, rows, columns] = leaves[8 * t + k, d].astype(F32)


def finish(x, early, leaves):
    return pl.pallas_call(
        finish_kernel,
        out_shape=[
            jax.ShapeDtypeStruct((7, 64, 1024), F32),
            jax.ShapeDtypeStruct((64, 1024), F32),
        ],
        in_specs=[SMEM] + [pl.BlockSpec(memory_space=pltpu.VMEM)] * 5,
        compiler_params=params(),
        name="finish",
    )(x, *early, leaves)


def gather_rows(value):
    return lax.all_gather(value, "prow")


def per_device(right_sub, right_root, inverse_sub, inverse_root, factor_blocks, block_lists):
    position = lax.axis_index("prow").astype(jnp.int32)
    column = lax.axis_index("pcol").astype(jnp.int32)
    x = position[None]
    inverse_sub = inverse_sub.reshape(7, 8, 128, 128)
    sent, middle_weights, top_weights = start(
        (column % 8)[None],
        right_sub,
        right_root,
        inverse_sub,
        inverse_root.reshape(8, 128, 128),
        factor_blocks,
        block_lists.T,
    )
    middle_weights = gather_rows(middle_weights)
    top_weights = gather_rows(top_weights)

    got = lax.all_to_all(sent, "prow", 0, 0, tiled=True)
    fwd_leaf, crit, other, leaf_weights = leaf_update(x, got, inverse_sub, factor_blocks)
    leaf_weights = gather_rows(leaf_weights)
    crit = [crit[0]] + [shift(crit[d], d) for d in range(1, NX)]
    other = [other[0]] + [shift(other[d], d) for d in range(1, NX)]
    table = got[:, 24, 0:2, 0:17].astype(jnp.int32)
    right = lax.dynamic_index_in_dim(got, column // 8, 0, keepdims=False)
    right = right[16:20].astype(F32) + right[20:24].astype(F32)
    parts = leaf_spread(x, table, crit)

    values = gather_columns(right[1:3] - reduce_columns(parts))
    fwd_middle, parts, acc_root = middle_forward(x, table, values, middle_weights, other)
    values = gather_columns(right[0] - reduce_columns(parts))
    fwd_top, parts = top_forward(x, table, values, top_weights, acc_root)
    total = reduce_columns(parts)
    total = total + lax.ppermute(total, "layer", [(0, 1), (1, 0)])
    values = gather_columns(right[3] - total)
    root = gather_columns(reduce_columns(root_solve(values, top_weights)))
    parts = top_backward(x, table, root, fwd_top, top_weights)
    top = gather_columns(reduce_columns(parts))
    parts = middle_backward(x, table, root, top, fwd_middle, middle_weights)
    fwd_leaf = leaf_down(x, table, root, top, fwd_leaf, leaf_weights)
    middle = gather_columns(reduce_columns(parts))

    early = jnp.concatenate([root[:, None], top[:, None], middle], 1)
    pieces = []
    for d in range(NX):
        piece = lax.dynamic_slice_in_dim(early, 8 * lax.rem(position + d, NX), 8, 0)
        pieces.append(shift(piece, d) if d else piece)

    parts = leaf_backward(x, table, middle, fwd_leaf, leaf_weights)
    chunk = reduce_columns(parts).astype(BF)
    chunk = jnp.stack([chunk[0]] + [shift(chunk[d], d) for d in range(1, NX)])
    leaves = gather_columns(after(chunk, *pieces))
    return tuple(finish(x, pieces, leaves))


def solution(mesh):
    in_specs = (
        P("layer", None, "prow"),
        P(None, "prow"),
        P("layer", "prow", "pcol"),
        P("prow", "pcol"),
        P("layer", "pcol", "prow"),
        P("layer", "prow"),
    )
    out_specs = (P("layer", None, "prow"), P(None, "prow"))
    return jax.shard_map(
        per_device, mesh=mesh, in_specs=in_specs, out_specs=out_specs, check_vma=False
    )
```

```python
import jax
import jax.numpy as jnp
from jax import lax
from jax.experimental import pallas as pl
from jax.experimental.pallas import tpu as pltpu
from jax.sharding import PartitionSpec as P

NX = 4
NP = 32
RX = 16
BF = jnp.bfloat16
F32 = jnp.float32
LIMIT = 14 * 1024 * 1024
LARGE = 56 * 1024 * 1024

SMEM = pl.BlockSpec(memory_space=pltpu.SMEM)
VMEM = pl.BlockSpec(memory_space=pltpu.VMEM)
HBM = pl.BlockSpec(memory_space=pltpu.HBM)


def whole(*shape):
    return pl.BlockSpec(shape, lambda n: (0,) * len(shape))


def params(limit=LIMIT):
    return pltpu.CompilerParams(vmem_limit_bytes=limit)


def shift(value, distance):
    return lax.ppermute(value, "prow", [(i, (i + distance) % NX) for i in range(NX)])


def around(value):
    return [value] + [shift(value, distance) for distance in range(1, NX)]


def after(value, *earlier):
    return lax.optimization_barrier((value, *earlier))[0]


def exchange(value):
    return lax.all_to_all(value, "pcol", 0, 0, tiled=True)


def reduce_columns(parts):
    return jnp.sum(exchange(parts).astype(F32), axis=0)


def gather_columns(chunk):
    chunk = chunk.astype(BF)
    return exchange(jnp.broadcast_to(chunk[None], (NP,) + chunk.shape))


def dot(left, right):
    return lax.dot_general(left, right, (((1,), (0,)), ((), ())), preferred_element_type=F32)


def dot_t(left, right):
    return lax.dot_general(left, right, (((1,), (1,)), ((), ())), preferred_element_type=F32)


def row_start(x, distance):
    return pl.multiple_of(lax.rem(x + distance, NX) * RX, RX)


def source(x, distance):
    return lax.rem(x + (NX - distance), NX)


SENT = 25


def start_kernel(place, right_sub, right_root, inverse, inverse_root, factor, lists, sent, middle, top, rights, inverses, pieces, sems):
    column = place[0]

    def copy(source_ref, target_ref, index):
        pltpu.make_async_copy(source_ref, target_ref, sems.at[index]).start()

    copy(right_sub.at[3:7], rights, 0)
    copy(inverse.at[3:7], inverses, 1)
    columns = pl.ds(pl.multiple_of(128 * column, 128), 128)
    copy(right_sub.at[0:3, :, columns], pieces.at[0:3], 4)
    copy(right_root.at[:, columns], pieces.at[3], 4)

    def factor_copy(pair, target, first, index):
        for c in range(4):
            copy(factor.at[pair, :, 128 * c : 128 * (c + 1)], target.at[first + c], index)

    for m in range(2):
        copy(inverse.at[1 + m], middle.at[m, 0:8], 2)
        for i in range(2):
            factor_copy(1 + 2 * m + i, middle.at[m], 8 + 4 * i, 2)
    copy(inverse_root, top.at[0:8], 3)
    copy(inverse.at[0], top.at[8:16], 3)
    factor_copy(0, top, 16, 3)

    names = lists[...].astype(F32).astype(BF)
    pltpu.make_async_copy(pieces, pieces, sems.at[4]).wait()
    for r in range(NX):
        sent[r, 24] = jnp.zeros((RX, 128), BF)
        sent[r, 24, 0:2, 0:17] = names
        for t in range(4):
            piece = pieces[t, RX * r : RX * (r + 1), :]
            high = piece.astype(BF)
            sent[r, 16 + t] = high
            sent[r, 20 + t] = (piece - high.astype(F32)).astype(BF)
    pltpu.make_async_copy(rights, rights, sems.at[0]).wait()
    pltpu.make_async_copy(inverses, inverses, sems.at[1]).wait()
    for n in range(4):
        own = dot(rights[n].astype(BF), inverses[n].reshape(1024, 128)).astype(BF)
        for r in range(NX):
            for g in range(NX):
                sent[r, 4 * n + g] = own[RX * g : RX * (g + 1)]
    pltpu.make_async_copy(middle, middle, sems.at[2]).wait()
    pltpu.make_async_copy(top, top, sems.at[3]).wait()


def start(place, right_sub, right_root, inverse, inverse_root, factor, lists):
    hbm = pl.BlockSpec(memory_space=pl.ANY)
    return pl.pallas_call(
        start_kernel,
        out_shape=[
            jax.ShapeDtypeStruct((NX, SENT, RX, 128), BF),
            jax.ShapeDtypeStruct((2, 16, 128, 128), BF),
            jax.ShapeDtypeStruct((20, 128, 128), BF),
        ],
        in_specs=[SMEM] + [hbm] * 5 + [VMEM],
        out_specs=[VMEM] * 3,
        scratch_shapes=[
            pltpu.VMEM((4, 64, 1024), F32),
            pltpu.VMEM((4, 8, 128, 128), BF),
            pltpu.VMEM((4, 64, 128), F32),
            pltpu.SemaphoreType.DMA((5,)),
        ],
        compiler_params=params(LARGE),
        name="start",
    )(place, right_sub, right_root, inverse, inverse_root, factor, lists)


def leaf_update_kernel(x_ref, got, inverse, f0, f1, f2, fwd, *rest):
    crit, other, packed = rest[0:4], rest[4:8], rest[8]
    x, n = x_ref[0], pl.program_id(0)

    def total(d):
        tile = 4 * n + lax.rem(x + d, NX)
        parts = [got[r, tile].astype(F32) for r in range(NX)]
        return (parts[0] + parts[1]) + (parts[2] + parts[3])

    solved = [total(d) for d in range(NX)]
    fwd[n] = solved[0]
    left = jnp.concatenate(solved, axis=0).astype(BF)
    packed[0, 0:8] = inverse[0]
    for i, factor in enumerate((f0, f1, f2)):
        first = (12, 16, 8)[i]
        for c in range(4):
            packed[0, first + c] = factor[0, :, 128 * c : 128 * (c + 1)]
        update = dot(left, factor[0]).astype(BF)
        for d in range(NX):
            piece = update[RX * d : RX * (d + 1)]
            if i == 2:
                crit[d][n] = piece
            else:
                other[d][2 * n + i] = piece


def leaf_update(x, got, inverse, factor):
    result = pl.pallas_call(
        leaf_update_kernel,
        grid=(4,),
        out_shape=[jax.ShapeDtypeStruct((4, RX, 128), F32)]
        + [jax.ShapeDtypeStruct((4, RX, 512), BF)] * 4
        + [jax.ShapeDtypeStruct((8, RX, 512), BF)] * 4
        + [jax.ShapeDtypeStruct((4, 20, 128, 128), BF)],
        in_specs=[
            SMEM,
            whole(NX, SENT, RX, 128),
            pl.BlockSpec((1, 8, 128, 128), lambda n: (3 + n, 0, 0, 0)),
        ]
        + [pl.BlockSpec((1, 128, 512), lambda n, i=i: (5 + 3 * n + i, 0, 0)) for i in range(3)],
        out_specs=[whole(4, RX, 128)]
        + [whole(4, RX, 512)] * 4
        + [whole(8, RX, 512)] * 4
        + [pl.BlockSpec((1, 20, 128, 128), lambda n: (n, 0, 0, 0))],
        compiler_params=params(LARGE),
        name="leaf_update",
    )(x, got, inverse, factor, factor, factor)
    return result[0], result[1:5], result[5:9], result[9]


def listed(table, r, pair, j):
    return table[r, j, pair]


def add_update(acc, table, r, pair, update, *lead):
    for j in range(2):
        block = listed(table, r, pair, j)
        for h in range(2):
            index = (2 * block + h, *lead)
            tile = update[:, 256 * j + 128 * h : 256 * j + 128 * (h + 1)]
            acc[index] = acc[index] + tile.astype(F32)


def leaf_spread_kernel(x_ref, table, c0, c1, c2, c3, out, acc):
    x = x_ref[0]
    acc[...] = jnp.zeros(acc.shape, F32)
    for d, crit in enumerate((c0, c1, c2, c3)):
        for n in range(4):
            add_update(acc, table, source(x, d), 5 + 3 * n + 2, crit[n], n // 2)
    out[...] = acc[...].astype(BF)


def leaf_spread(x, table, crit):
    return pl.pallas_call(
        leaf_spread_kernel,
        out_shape=jax.ShapeDtypeStruct((NP, 2, RX, 128), BF),
        in_specs=[SMEM] * 2 + [VMEM] * 4,
        scratch_shapes=[pltpu.VMEM((NP, 2, RX, 128), F32)],
        compiler_params=params(),
        name="leaf_spread",
    )(x, table, *crit)


def fetch(weights, near, sems, nodes, tiles):
    moves = [
        [
            pltpu.make_async_copy(
                weights.at[r, n, 0:tiles], near.at[r, n], sems.at[NX * n + r]
            )
            for r in range(NX)
        ]
        for n in range(nodes)
    ]
    for node in moves:
        for move in node:
            move.start()
    return moves


def inverse_share(tiles):
    return tiles.reshape(1024, 128)


def factor_share(tiles):
    return jnp.concatenate([tiles[c] for c in range(4)], axis=1)


def solve_columns(values, inverse, *lead):
    total = None
    for r in range(NX):
        left = jnp.concatenate([values[(8 * r + k, *lead)] for k in range(8)], axis=1)
        term = dot(left, inverse(r))
        total = term if total is None else total + term
    return total


def solve_rows(target, inverse, store):
    for r in range(NX):
        wide = dot_t(target, inverse(r)).astype(BF)
        for k in range(8):
            store(r, k, wide[:, 128 * k : 128 * (k + 1)])


def multiply_update(acc, x, table, pair, rounded, factor, *lead):
    for r in range(NX):
        update = dot(rounded, factor(r))
        add_update(acc, table, r, pair, update, *lead)


def pick_product(x, table, pair, values, factor, *lead):
    total = None
    for r in range(NX):
        tiles = []
        for j in range(2):
            block = listed(table, r, pair, j)
            tiles += [values[(2 * block, *lead)], values[(2 * block + 1, *lead)]]
        term = dot_t(jnp.concatenate(tiles, axis=1), factor(r))
        total = term if total is None else total + term
    return total


TILES = whole(NP, RX, 128)
TOP_INVERSE = pl.BlockSpec((NX, 8, 128, 128), lambda n: (0, 1, 0, 0))
TOP_FACTOR = pl.BlockSpec((NX, 4, 128, 128), lambda n: (0, 4, 0, 0))


def middle_inverse(weights, m):
    return lambda r: inverse_share(weights[r, m, 0:8])


def middle_factor(weights, m, i):
    return lambda r: factor_share(weights[r, m, 8 + 4 * i : 12 + 4 * i])


def middle_forward_kernel(x_ref, table, values, far, o0, o1, o2, o3, fwd, out, acc_root, acc, weights, sems):
    x = x_ref[0]
    moves = fetch(far, weights, sems, 2, 16)
    acc[...] = jnp.zeros(acc.shape, F32)
    acc_root[...] = jnp.zeros(acc_root.shape, F32)
    for d, other in enumerate((o0, o1, o2, o3)):
        for n in range(4):
            r = source(x, d)
            add_update(acc_root, table, r, 5 + 3 * n, other[2 * n])
            add_update(acc, table, r, 5 + 3 * n + 1, other[2 * n + 1])
    for m in range(2):
        for move in moves[m]:
            move.wait()
        solved = solve_columns(values, middle_inverse(weights, m), m)
        fwd[m] = solved
        rounded = solved.astype(BF)
        multiply_update(acc_root, x, table, 1 + 2 * m, rounded, middle_factor(weights, m, 0))
        multiply_update(acc, x, table, 2 + 2 * m, rounded, middle_factor(weights, m, 1))
    out[...] = acc[...].astype(BF)


def middle_forward(x, table, values, weights, other):
    return pl.pallas_call(
        middle_forward_kernel,
        out_shape=[
            jax.ShapeDtypeStruct((2, RX, 128), F32),
            jax.ShapeDtypeStruct((NP, RX, 128), BF),
            jax.ShapeDtypeStruct((NP, RX, 128), F32),
        ],
        in_specs=[SMEM] * 2 + [VMEM, HBM] + [VMEM] * 4,
        scratch_shapes=[
            pltpu.VMEM((NP, RX, 128), F32),
            pltpu.VMEM((NX, 2, 16, 128, 128), BF),
            pltpu.SemaphoreType.DMA((2 * NX,)),
        ],
        compiler_params=params(LARGE),
        name="middle_forward",
    )(x, table, values, weights, *other)


def top_forward_kernel(x_ref, table, values, inverse, factor, acc_in, fwd, out, acc):
    acc[...] = acc_in[...]
    solved = solve_columns(values, lambda r: inverse_share(inverse[r]))
    fwd[...] = solved
    multiply_update(
        acc, x_ref[0], table, 0, solved.astype(BF), lambda r: factor_share(factor[r])
    )
    out[...] = acc[...].astype(BF)


def top_forward(x, table, values, weights, acc_root):
    return pl.pallas_call(
        top_forward_kernel,
        grid=(1,),
        out_shape=[
            jax.ShapeDtypeStruct((RX, 128), F32),
            jax.ShapeDtypeStruct((NP, RX, 128), BF),
        ],
        in_specs=[SMEM] * 2 + [TILES, TOP_INVERSE, TOP_FACTOR, TILES],
        out_specs=[whole(RX, 128), TILES],
        scratch_shapes=[pltpu.VMEM((NP, RX, 128), F32)],
        compiler_params=params(),
        name="top_forward",
    )(x, table, values, weights, weights, acc_root)


def root_kernel(values, weights, out):
    inverse = lambda r: inverse_share(weights[r])
    rounded = solve_columns(values, inverse).astype(BF)

    def store(r, k, tile):
        out[8 * r + k] = tile

    solve_rows(rounded, inverse, store)


def root_solve(values, weights):
    return pl.pallas_call(
        root_kernel,
        grid=(1,),
        out_shape=jax.ShapeDtypeStruct((NP, RX, 128), BF),
        in_specs=[TILES, whole(NX, 8, 128, 128)],
        out_specs=TILES,
        compiler_params=params(),
        name="root_solve",
    )(values, weights)


def top_backward_kernel(x_ref, table, root, fwd, inverse, factor, out):
    down = pick_product(x_ref[0], table, 0, root, lambda r: factor_share(factor[r]))

    def store(r, k, tile):
        out[8 * r + k] = tile

    solve_rows((fwd[...] - down).astype(BF), lambda r: inverse_share(inverse[r]), store)


def top_backward(x, table, root, fwd, weights):
    return pl.pallas_call(
        top_backward_kernel,
        grid=(1,),
        out_shape=jax.ShapeDtypeStruct((NP, RX, 128), BF),
        in_specs=[SMEM] * 2 + [TILES, whole(RX, 128), TOP_INVERSE, TOP_FACTOR],
        out_specs=TILES,
        compiler_params=params(),
        name="top_backward",
    )(x, table, root, fwd, weights, weights)


def middle_backward_kernel(x_ref, table, root, top, fwd, far, out, weights, sems):
    x = x_ref[0]
    moves = fetch(far, weights, sems, 2, 16)
    for m in range(2):
        for move in moves[m]:
            move.wait()
        down = pick_product(x, table, 1 + 2 * m, root, middle_factor(weights, m, 0))
        down = down + pick_product(x, table, 2 + 2 * m, top, middle_factor(weights, m, 1))

        def store(r, k, tile, m=m):
            out[8 * r + k, m] = tile

        solve_rows((fwd[m] - down).astype(BF), middle_inverse(weights, m), store)


def middle_backward(x, table, root, top, fwd, weights):
    return pl.pallas_call(
        middle_backward_kernel,
        out_shape=jax.ShapeDtypeStruct((NP, 2, RX, 128), BF),
        in_specs=[SMEM] * 2 + [VMEM] * 3 + [HBM],
        scratch_shapes=[
            pltpu.VMEM((NX, 2, 16, 128, 128), BF),
            pltpu.SemaphoreType.DMA((2 * NX,)),
        ],
        compiler_params=params(LARGE),
        name="middle_backward",
    )(x, table, root, top, fwd, weights)


def leaf_down_kernel(x_ref, table, root, top, fwd, to_root, to_top, out):
    x = x_ref[0]
    first = 5 + 3 * pl.program_id(0)
    down = pick_product(x, table, first, root, lambda r: factor_share(to_root[r, 0]))
    down = down + pick_product(x, table, first + 1, top, lambda r: factor_share(to_top[r, 0]))
    out[0] = fwd[0] - down


def leaf_down(x, table, root, top, fwd, weights):
    factor_at = lambda i: pl.BlockSpec((NX, 1, 4, 128, 128), lambda n: (0, n, i, 0, 0))
    return pl.pallas_call(
        leaf_down_kernel,
        grid=(4,),
        out_shape=jax.ShapeDtypeStruct((4, RX, 128), F32),
        in_specs=[SMEM] * 2
        + [TILES, TILES, pl.BlockSpec((1, RX, 128), lambda n: (n, 0, 0)), factor_at(3), factor_at(4)],
        out_specs=pl.BlockSpec((1, RX, 128), lambda n: (n, 0, 0)),
        compiler_params=params(LARGE),
        name="leaf_down",
    )(x, table, root, top, fwd, weights, weights)


def leaf_backward_kernel(x_ref, table, middle, fwd, far, out, near, sems):
    x = x_ref[0]
    moves = fetch(far, near, sems, 4, 12)
    for n in range(4):
        for move in moves[n]:
            move.wait()
        down = pick_product(
            x, table, 7 + 3 * n, middle, lambda r: factor_share(near[r, n, 8:12]), n // 2
        )

        def store(r, k, tile, n=n):
            out[8 * n + k, lax.rem(r + NX - x, NX)] = tile

        target = (fwd[n] - down).astype(BF)
        solve_rows(target, lambda r: inverse_share(near[r, n, 0:8]), store)


def leaf_backward(x, table, middle, fwd, weights):
    return pl.pallas_call(
        leaf_backward_kernel,
        out_shape=jax.ShapeDtypeStruct((NP, NX, RX, 128), BF),
        in_specs=[SMEM] * 2 + [VMEM] * 2 + [HBM],
        scratch_shapes=[
            pltpu.VMEM((NX, 4, 12, 128, 128), BF),
            pltpu.SemaphoreType.DMA((4 * NX,)),
        ],
        compiler_params=params(LARGE),
        name="leaf_backward",
    )(x, table, middle, fwd, weights)


def finish_kernel(x_ref, e0, e1, e2, e3, leaves, out_sub, out_root):
    x = x_ref[0]
    for d, early in enumerate((e0, e1, e2, e3)):
        rows = pl.ds(pl.multiple_of(RX * source(x, d), RX), RX)
        for k in range(8):
            columns = slice(128 * k, 128 * (k + 1))
            out_root[rows, columns] = early[k, 0].astype(F32)
            for t in range(3):
                out_sub[t, rows, columns] = early[k, 1 + t].astype(F32)
            for t in range(4):
                out_sub[3 + t, rows, columns] = leaves[8 * t + k, d].astype(F32)


def finish(x, early, leaves):
    return pl.pallas_call(
        finish_kernel,
        out_shape=[
            jax.ShapeDtypeStruct((7, 64, 1024), F32),
            jax.ShapeDtypeStruct((64, 1024), F32),
        ],
        in_specs=[SMEM] + [pl.BlockSpec(memory_space=pltpu.VMEM)] * 5,
        compiler_params=params(),
        name="finish",
    )(x, *early, leaves)


def gather_rows(value):
    return lax.all_gather(value, "prow")


def per_device(right_sub, right_root, inverse_sub, inverse_root, factor_blocks, block_lists):
    position = lax.axis_index("prow").astype(jnp.int32)
    column = lax.axis_index("pcol").astype(jnp.int32)
    x = position[None]
    inverse_sub = inverse_sub.reshape(7, 8, 128, 128)
    sent, middle_weights, top_weights = start(
        (column % 8)[None],
        right_sub,
        right_root,
        inverse_sub,
        inverse_root.reshape(8, 128, 128),
        factor_blocks,
        block_lists.T,
    )
    middle_weights = gather_rows(middle_weights)
    top_weights = gather_rows(top_weights)

    got = lax.all_to_all(sent, "prow", 0, 0, tiled=True)
    fwd_leaf, crit, other, leaf_weights = leaf_update(x, got, inverse_sub, factor_blocks)
    leaf_weights = gather_rows(leaf_weights)
    crit = [crit[0]] + [shift(crit[d], d) for d in range(1, NX)]
    other = [other[0]] + [shift(other[d], d) for d in range(1, NX)]
    table = got[:, 24, 0:2, 0:17].astype(jnp.int32)
    right = lax.dynamic_index_in_dim(got, column // 8, 0, keepdims=False)
    right = right[16:20].astype(F32) + right[20:24].astype(F32)
    parts = leaf_spread(x, table, crit)

    values = gather_columns(right[1:3] - reduce_columns(parts))
    fwd_middle, parts, acc_root = middle_forward(x, table, values, middle_weights, other)
    values = gather_columns(right[0] - reduce_columns(parts))
    fwd_top, parts = top_forward(x, table, values, top_weights, acc_root)
    total = reduce_columns(parts)
    total = total + lax.ppermute(total, "layer", [(0, 1), (1, 0)])
    values = gather_columns(right[3] - total)
    root = gather_columns(reduce_columns(root_solve(values, top_weights)))
    parts = top_backward(x, table, root, fwd_top, top_weights)
    top = gather_columns(reduce_columns(parts))
    parts = middle_backward(x, table, root, top, fwd_middle, middle_weights)
    fwd_leaf = leaf_down(x, table, root, top, fwd_leaf, leaf_weights)
    middle = gather_columns(reduce_columns(parts))

    early = jnp.concatenate([root[:, None], top[:, None], middle], 1)
    pieces = []
    for d in range(NX):
        piece = lax.dynamic_slice_in_dim(early, 8 * lax.rem(position + d, NX), 8, 0)
        pieces.append(shift(piece, d) if d else piece)

    parts = leaf_backward(x, table, middle, fwd_leaf, leaf_weights)
    chunk = reduce_columns(parts).astype(BF)
    chunk = jnp.stack([chunk[0]] + [shift(chunk[d], d) for d in range(1, NX)])
    leaves = gather_columns(after(chunk, *pieces))
    return tuple(finish(x, pieces, leaves))


def solution(mesh):
    in_specs = (
        P("layer", None, "prow"),
        P(None, "prow"),
        P("layer", "prow", "pcol"),
        P("prow", "pcol"),
        P("layer", "pcol", "prow"),
        P("layer", "prow"),
    )
    out_specs = (P("layer", None, "prow"), P(None, "prow"))
    return jax.shard_map(
        per_device, mesh=mesh, in_specs=in_specs, out_specs=out_specs, check_vma=False
    )
```

```python
import jax
import jax.numpy as jnp
from jax import lax
from jax.experimental import pallas as pl
from jax.experimental.pallas import tpu as pltpu
from jax.sharding import PartitionSpec as P

NX = 4
NP = 32
RX = 16
BF = jnp.bfloat16
F32 = jnp.float32
LIMIT = 14 * 1024 * 1024
LARGE = 56 * 1024 * 1024

SMEM = pl.BlockSpec(memory_space=pltpu.SMEM)
VMEM = pl.BlockSpec(memory_space=pltpu.VMEM)


def whole(*shape):
    return pl.BlockSpec(shape, lambda n: (0,) * len(shape))


def params(limit=LIMIT):
    return pltpu.CompilerParams(vmem_limit_bytes=limit)


def shift(value, distance):
    return lax.ppermute(value, "prow", [(i, (i + distance) % NX) for i in range(NX)])


def around(value):
    return [value] + [shift(value, distance) for distance in range(1, NX)]


def after(value, *earlier):
    return lax.optimization_barrier((value, *earlier))[0]


def exchange(value):
    return lax.all_to_all(value, "pcol", 0, 0, tiled=True)


def reduce_columns(parts):
    return jnp.sum(exchange(parts).astype(F32), axis=0)


def gather_columns(chunk):
    chunk = chunk.astype(BF)
    return exchange(jnp.broadcast_to(chunk[None], (NP,) + chunk.shape))


def dot(left, right):
    return lax.dot_general(left, right, (((1,), (0,)), ((), ())), preferred_element_type=F32)


def dot_t(left, right):
    return lax.dot_general(left, right, (((1,), (1,)), ((), ())), preferred_element_type=F32)


def row_start(x, distance):
    return pl.multiple_of(lax.rem(x + distance, NX) * RX, RX)


def source(x, distance):
    return lax.rem(x + (NX - distance), NX)


SENT = 25


def start_kernel(place, right_sub, right_root, inverse, inverse_root, factor, lists, sent, middle, top, rights, inverses, pieces, sems):
    column = place[0]

    def copy(source_ref, target_ref, index):
        pltpu.make_async_copy(source_ref, target_ref, sems.at[index]).start()

    copy(right_sub.at[3:7], rights, 0)
    copy(inverse.at[3:7], inverses, 1)
    columns = pl.ds(pl.multiple_of(128 * column, 128), 128)
    copy(right_sub.at[0:3, :, columns], pieces.at[0:3], 4)
    copy(right_root.at[:, columns], pieces.at[3], 4)

    def factor_copy(pair, target, first, index):
        for c in range(4):
            copy(factor.at[pair, :, 128 * c : 128 * (c + 1)], target.at[first + c], index)

    for m in range(2):
        copy(inverse.at[1 + m], middle.at[m, 0:8], 2)
        for i in range(2):
            factor_copy(1 + 2 * m + i, middle.at[m], 8 + 4 * i, 2)
    copy(inverse_root, top.at[0:8], 3)
    copy(inverse.at[0], top.at[8:16], 3)
    factor_copy(0, top, 16, 3)

    names = lists[...].astype(F32).astype(BF)
    pltpu.make_async_copy(pieces, pieces, sems.at[4]).wait()
    for r in range(NX):
        sent[r, 24] = jnp.zeros((RX, 128), BF)
        sent[r, 24, 0:2, 0:17] = names
        for t in range(4):
            piece = pieces[t, RX * r : RX * (r + 1), :]
            high = piece.astype(BF)
            sent[r, 16 + t] = high
            sent[r, 20 + t] = (piece - high.astype(F32)).astype(BF)
    pltpu.make_async_copy(rights, rights, sems.at[0]).wait()
    pltpu.make_async_copy(inverses, inverses, sems.at[1]).wait()
    for n in range(4):
        own = dot(rights[n].astype(BF), inverses[n].reshape(1024, 128)).astype(BF)
        for r in range(NX):
            for g in range(NX):
                sent[r, 4 * n + g] = own[RX * g : RX * (g + 1)]
    pltpu.make_async_copy(middle, middle, sems.at[2]).wait()
    pltpu.make_async_copy(top, top, sems.at[3]).wait()


def start(place, right_sub, right_root, inverse, inverse_root, factor, lists):
    hbm = pl.BlockSpec(memory_space=pl.ANY)
    return pl.pallas_call(
        start_kernel,
        out_shape=[
            jax.ShapeDtypeStruct((NX, SENT, RX, 128), BF),
            jax.ShapeDtypeStruct((2, 16, 128, 128), BF),
            jax.ShapeDtypeStruct((20, 128, 128), BF),
        ],
        in_specs=[SMEM] + [hbm] * 5 + [VMEM],
        out_specs=[VMEM] * 3,
        scratch_shapes=[
            pltpu.VMEM((4, 64, 1024), F32),
            pltpu.VMEM((4, 8, 128, 128), BF),
            pltpu.VMEM((4, 64, 128), F32),
            pltpu.SemaphoreType.DMA((5,)),
        ],
        compiler_params=params(LARGE),
        name="start",
    )(place, right_sub, right_root, inverse, inverse_root, factor, lists)


def leaf_update_kernel(x_ref, got, inverse, f0, f1, f2, fwd, *rest):
    crit, other, packed = rest[0:4], rest[4:8], rest[8]
    x, n = x_ref[0], pl.program_id(0)

    def total(d):
        tile = 4 * n + lax.rem(x + d, NX)
        parts = [got[r, tile].astype(F32) for r in range(NX)]
        return (parts[0] + parts[1]) + (parts[2] + parts[3])

    solved = [total(d) for d in range(NX)]
    fwd[n] = solved[0]
    left = jnp.concatenate(solved, axis=0).astype(BF)
    packed[0, 0:8] = inverse[0]
    for i, factor in enumerate((f0, f1, f2)):
        first = (12, 16, 8)[i]
        for c in range(4):
            packed[0, first + c] = factor[0, :, 128 * c : 128 * (c + 1)]
        update = dot(left, factor[0]).astype(BF)
        for d in range(NX):
            piece = update[RX * d : RX * (d + 1)]
            if i == 2:
                crit[d][n] = piece
            else:
                other[d][2 * n + i] = piece


def leaf_update(x, got, inverse, factor):
    result = pl.pallas_call(
        leaf_update_kernel,
        grid=(4,),
        out_shape=[jax.ShapeDtypeStruct((4, RX, 128), F32)]
        + [jax.ShapeDtypeStruct((4, RX, 512), BF)] * 4
        + [jax.ShapeDtypeStruct((8, RX, 512), BF)] * 4
        + [jax.ShapeDtypeStruct((4, 20, 128, 128), BF)],
        in_specs=[
            SMEM,
            whole(NX, SENT, RX, 128),
            pl.BlockSpec((1, 8, 128, 128), lambda n: (3 + n, 0, 0, 0)),
        ]
        + [pl.BlockSpec((1, 128, 512), lambda n, i=i: (5 + 3 * n + i, 0, 0)) for i in range(3)],
        out_specs=[whole(4, RX, 128)]
        + [whole(4, RX, 512)] * 4
        + [whole(8, RX, 512)] * 4
        + [pl.BlockSpec((1, 20, 128, 128), lambda n: (n, 0, 0, 0))],
        compiler_params=params(LARGE),
        name="leaf_update",
    )(x, got, inverse, factor, factor, factor)
    return result[0], result[1:5], result[5:9], result[9]


def listed(table, r, pair, j):
    return table[r, j, pair]


def add_update(acc, table, r, pair, update, *lead):
    for j in range(2):
        block = listed(table, r, pair, j)
        index = (pl.ds(2 * block, 2), *lead)
        tiles = [update[:, 256 * j + 128 * h : 256 * j + 128 * (h + 1)] for h in range(2)]
        acc[index] = acc[index] + jnp.stack(tiles).astype(F32)


def leaf_spread_kernel(x_ref, table, c0, c1, c2, c3, out, acc):
    x = x_ref[0]
    acc[...] = jnp.zeros(acc.shape, F32)
    for d, crit in enumerate((c0, c1, c2, c3)):
        for n in range(4):
            add_update(acc, table, source(x, d), 5 + 3 * n + 2, crit[n], n // 2)
    out[...] = acc[...].astype(BF)


def leaf_spread(x, table, crit):
    return pl.pallas_call(
        leaf_spread_kernel,
        out_shape=jax.ShapeDtypeStruct((NP, 2, RX, 128), BF),
        in_specs=[SMEM] * 2 + [VMEM] * 4,
        scratch_shapes=[pltpu.VMEM((NP, 2, RX, 128), F32)],
        compiler_params=params(),
        name="leaf_spread",
    )(x, table, *crit)


def inverse_share(tiles):
    return tiles.reshape(1024, 128)


def factor_share(tiles):
    return jnp.concatenate([tiles[c] for c in range(4)], axis=1)


def solve_columns(values, inverse, *lead):
    total = None
    for r in range(NX):
        left = jnp.concatenate([values[(8 * r + k, *lead)] for k in range(8)], axis=1)
        term = dot(left, inverse(r))
        total = term if total is None else total + term
    return total


def solve_rows(target, inverse, store):
    for r in range(NX):
        wide = dot_t(target, inverse(r)).astype(BF)
        for k in range(8):
            store(r, k, wide[:, 128 * k : 128 * (k + 1)])


def multiply_update(acc, x, table, pair, rounded, factor, *lead):
    for r in range(NX):
        update = dot(rounded, factor(r))
        add_update(acc, table, r, pair, update, *lead)


def pick_product(x, table, pair, values, factor, *lead):
    total = None
    for r in range(NX):
        tiles = []
        for j in range(2):
            block = listed(table, r, pair, j)
            pair_of_tiles = values[(pl.ds(2 * block, 2), *lead)]
            tiles += [pair_of_tiles[0], pair_of_tiles[1]]
        term = dot_t(jnp.concatenate(tiles, axis=1), factor(r))
        total = term if total is None else total + term
    return total


TILES = whole(NP, RX, 128)
TOP_INVERSE = pl.BlockSpec((NX, 8, 128, 128), lambda n: (0, 1, 0, 0))
TOP_FACTOR = pl.BlockSpec((NX, 4, 128, 128), lambda n: (0, 4, 0, 0))


def middle_inverse(weights, m):
    return lambda r: inverse_share(weights[r, m, 0:8])


def middle_factor(weights, m, i):
    return lambda r: factor_share(weights[r, m, 8 + 4 * i : 12 + 4 * i])


def middle_forward_kernel(x_ref, table, values, weights, o0, o1, o2, o3, fwd, out, acc_root, acc):
    x = x_ref[0]
    acc[...] = jnp.zeros(acc.shape, F32)
    acc_root[...] = jnp.zeros(acc_root.shape, F32)
    for d, other in enumerate((o0, o1, o2, o3)):
        for n in range(4):
            r = source(x, d)
            add_update(acc_root, table, r, 5 + 3 * n, other[2 * n])
            add_update(acc, table, r, 5 + 3 * n + 1, other[2 * n + 1])
    for m in range(2):
        solved = solve_columns(values, middle_inverse(weights, m), m)
        fwd[m] = solved
        rounded = solved.astype(BF)
        multiply_update(acc_root, x, table, 1 + 2 * m, rounded, middle_factor(weights, m, 0))
        multiply_update(acc, x, table, 2 + 2 * m, rounded, middle_factor(weights, m, 1))
    out[...] = acc[...].astype(BF)


def middle_forward(x, table, values, weights, other):
    return pl.pallas_call(
        middle_forward_kernel,
        out_shape=[
            jax.ShapeDtypeStruct((2, RX, 128), F32),
            jax.ShapeDtypeStruct((NP, RX, 128), BF),
            jax.ShapeDtypeStruct((NP, RX, 128), F32),
        ],
        in_specs=[SMEM] * 2 + [VMEM] * 6,
        scratch_shapes=[pltpu.VMEM((NP, RX, 128), F32)],
        compiler_params=params(),
        name="middle_forward",
    )(x, table, values, weights, *other)


def top_forward_kernel(x_ref, table, values, inverse, factor, acc_in, fwd, out, acc):
    acc[...] = acc_in[...]
    solved = solve_columns(values, lambda r: inverse_share(inverse[r]))
    fwd[...] = solved
    multiply_update(
        acc, x_ref[0], table, 0, solved.astype(BF), lambda r: factor_share(factor[r])
    )
    out[...] = acc[...].astype(BF)


def top_forward(x, table, values, weights, acc_root):
    return pl.pallas_call(
        top_forward_kernel,
        grid=(1,),
        out_shape=[
            jax.ShapeDtypeStruct((RX, 128), F32),
            jax.ShapeDtypeStruct((NP, RX, 128), BF),
        ],
        in_specs=[SMEM] * 2 + [TILES, TOP_INVERSE, TOP_FACTOR, TILES],
        out_specs=[whole(RX, 128), TILES],
        scratch_shapes=[pltpu.VMEM((NP, RX, 128), F32)],
        compiler_params=params(),
        name="top_forward",
    )(x, table, values, weights, weights, acc_root)


def root_kernel(values, weights, out):
    inverse = lambda r: inverse_share(weights[r])
    rounded = solve_columns(values, inverse).astype(BF)

    def store(r, k, tile):
        out[8 * r + k] = tile

    solve_rows(rounded, inverse, store)


def root_solve(values, weights):
    return pl.pallas_call(
        root_kernel,
        grid=(1,),
        out_shape=jax.ShapeDtypeStruct((NP, RX, 128), BF),
        in_specs=[TILES, whole(NX, 8, 128, 128)],
        out_specs=TILES,
        compiler_params=params(),
        name="root_solve",
    )(values, weights)


def top_backward_kernel(x_ref, table, root, fwd, inverse, factor, out):
    down = pick_product(x_ref[0], table, 0, root, lambda r: factor_share(factor[r]))

    def store(r, k, tile):
        out[8 * r + k] = tile

    solve_rows((fwd[...] - down).astype(BF), lambda r: inverse_share(inverse[r]), store)


def top_backward(x, table, root, fwd, weights):
    return pl.pallas_call(
        top_backward_kernel,
        grid=(1,),
        out_shape=jax.ShapeDtypeStruct((NP, RX, 128), BF),
        in_specs=[SMEM] * 2 + [TILES, whole(RX, 128), TOP_INVERSE, TOP_FACTOR],
        out_specs=TILES,
        compiler_params=params(),
        name="top_backward",
    )(x, table, root, fwd, weights, weights)


def middle_backward_kernel(x_ref, table, root, top, fwd, weights, out):
    x = x_ref[0]
    for m in range(2):
        down = pick_product(x, table, 1 + 2 * m, root, middle_factor(weights, m, 0))
        down = down + pick_product(x, table, 2 + 2 * m, top, middle_factor(weights, m, 1))

        def store(r, k, tile, m=m):
            out[8 * r + k, m] = tile

        solve_rows((fwd[m] - down).astype(BF), middle_inverse(weights, m), store)


def middle_backward(x, table, root, top, fwd, weights):
    return pl.pallas_call(
        middle_backward_kernel,
        out_shape=jax.ShapeDtypeStruct((NP, 2, RX, 128), BF),
        in_specs=[SMEM] * 2 + [VMEM] * 4,
        compiler_params=params(LARGE),
        name="middle_backward",
    )(x, table, root, top, fwd, weights)


def leaf_down_kernel(x_ref, table, root, top, fwd, to_root, to_top, out):
    x = x_ref[0]
    first = 5 + 3 * pl.program_id(0)
    down = pick_product(x, table, first, root, lambda r: factor_share(to_root[r, 0]))
    down = down + pick_product(x, table, first + 1, top, lambda r: factor_share(to_top[r, 0]))
    out[0] = fwd[0] - down


def leaf_down(x, table, root, top, fwd, weights):
    factor_at = lambda i: pl.BlockSpec((NX, 1, 4, 128, 128), lambda n: (0, n, i, 0, 0))
    return pl.pallas_call(
        leaf_down_kernel,
        grid=(4,),
        out_shape=jax.ShapeDtypeStruct((4, RX, 128), F32),
        in_specs=[SMEM] * 2
        + [TILES, TILES, pl.BlockSpec((1, RX, 128), lambda n: (n, 0, 0)), factor_at(3), factor_at(4)],
        out_specs=pl.BlockSpec((1, RX, 128), lambda n: (n, 0, 0)),
        compiler_params=params(LARGE),
        name="leaf_down",
    )(x, table, root, top, fwd, weights, weights)


def leaf_backward_kernel(x_ref, table, middle, fwd, weights, out):
    x, n = x_ref[0], pl.program_id(0)
    down = pick_product(
        x, table, 7 + 3 * n, middle, lambda r: factor_share(weights[r, 0, 8:12]), n // 2
    )

    def store(r, k, tile):
        out[r, k] = tile

    inverse = lambda r: inverse_share(weights[r, 0, 0:8])
    solve_rows((fwd[0] - down).astype(BF), inverse, store)


def leaf_backward(x, table, middle, fwd, weights):
    return pl.pallas_call(
        leaf_backward_kernel,
        grid=(4,),
        out_shape=jax.ShapeDtypeStruct((NX, NP, RX, 128), BF),
        in_specs=[SMEM] * 2
        + [
            whole(NP, 2, RX, 128),
            pl.BlockSpec((1, RX, 128), lambda n: (n, 0, 0)),
            pl.BlockSpec((NX, 1, 12, 128, 128), lambda n: (0, n, 0, 0, 0)),
        ],
        out_specs=pl.BlockSpec((NX, 8, RX, 128), lambda n: (0, n, 0, 0)),
        compiler_params=params(LARGE),
        name="leaf_backward",
    )(x, table, middle, fwd, weights)


def finish_kernel(x_ref, e0, e1, e2, e3, leaves, out_sub, out_root):
    x = x_ref[0]
    for d, early in enumerate((e0, e1, e2, e3)):
        rows = pl.ds(pl.multiple_of(RX * source(x, d), RX), RX)
        for k in range(8):
            columns = slice(128 * k, 128 * (k + 1))
            out_root[rows, columns] = early[k, 0].astype(F32)
            for t in range(3):
                out_sub[t, rows, columns] = early[k, 1 + t].astype(F32)
            for t in range(4):
                tile = leaves[8 * t + k, d].astype(F32)
                out_sub[3 + t, RX * d : RX * (d + 1), columns] = tile


def finish(x, early, leaves):
    return pl.pallas_call(
        finish_kernel,
        out_shape=[
            jax.ShapeDtypeStruct((7, 64, 1024), F32),
            jax.ShapeDtypeStruct((64, 1024), F32),
        ],
        in_specs=[SMEM] + [pl.BlockSpec(memory_space=pltpu.VMEM)] * 5,
        compiler_params=params(),
        name="finish",
    )(x, *early, leaves)


def gather_rows(value):
    return lax.all_gather(value, "prow")


def per_device(right_sub, right_root, inverse_sub, inverse_root, factor_blocks, block_lists):
    position = lax.axis_index("prow").astype(jnp.int32)
    column = lax.axis_index("pcol").astype(jnp.int32)
    x = position[None]
    inverse_sub = inverse_sub.reshape(7, 8, 128, 128)
    sent, middle_weights, top_weights = start(
        (column % 8)[None],
        right_sub,
        right_root,
        inverse_sub,
        inverse_root.reshape(8, 128, 128),
        factor_blocks,
        block_lists.T,
    )
    middle_weights = gather_rows(middle_weights)
    top_weights = gather_rows(top_weights)

    got = lax.all_to_all(sent, "prow", 0, 0, tiled=True)
    fwd_leaf, crit, other, leaf_weights = leaf_update(x, got, inverse_sub, factor_blocks)
    leaf_weights = gather_rows(leaf_weights)
    crit = [crit[0]] + [shift(crit[d], d) for d in range(1, NX)]
    other = [other[0]] + [shift(other[d], d) for d in range(1, NX)]
    table = got[:, 24, 0:2, 0:17].astype(jnp.int32)
    right = lax.dynamic_index_in_dim(got, column // 8, 0, keepdims=False)
    right = right[16:20].astype(F32) + right[20:24].astype(F32)
    parts = leaf_spread(x, table, crit)

    values = gather_columns(right[1:3] - reduce_columns(parts))
    fwd_middle, parts, acc_root = middle_forward(x, table, values, middle_weights, other)
    values = gather_columns(right[0] - reduce_columns(parts))
    fwd_top, parts = top_forward(x, table, values, top_weights, acc_root)
    total = reduce_columns(parts)
    total = total + lax.ppermute(total, "layer", [(0, 1), (1, 0)])
    values = gather_columns(right[3] - total)
    root = gather_columns(reduce_columns(root_solve(values, top_weights)))
    parts = top_backward(x, table, root, fwd_top, top_weights)
    top = gather_columns(reduce_columns(parts))
    parts = middle_backward(x, table, root, top, fwd_middle, middle_weights)
    fwd_leaf = leaf_down(x, table, root, top, fwd_leaf, leaf_weights)
    middle = gather_columns(reduce_columns(parts))

    early = jnp.concatenate([root[:, None], top[:, None], middle], 1)
    pieces = []
    for d in range(NX):
        piece = lax.dynamic_slice_in_dim(early, 8 * lax.rem(position + d, NX), 8, 0)
        pieces.append(shift(piece, d) if d else piece)

    parts = leaf_backward(x, table, middle, fwd_leaf, leaf_weights)
    parts = lax.all_to_all(
        parts.reshape(NX * NP, RX, 128), ("prow", "pcol"), 0, 0, tiled=True
    ).reshape(NX, NP, RX, 128)
    chunk = jnp.sum(parts.astype(F32), axis=1).astype(BF)
    leaves = gather_columns(after(chunk, *pieces))
    return tuple(finish(x, pieces, leaves))


def solution(mesh):
    in_specs = (
        P("layer", None, "prow"),
        P(None, "prow"),
        P("layer", "prow", "pcol"),
        P("prow", "pcol"),
        P("layer", "pcol", "prow"),
        P("layer", "prow"),
    )
    out_specs = (P("layer", None, "prow"), P(None, "prow"))
    return jax.shard_map(
        per_device, mesh=mesh, in_specs=in_specs, out_specs=out_specs, check_vma=False
    )
```

```python
import jax
import jax.numpy as jnp
from jax import lax
from jax.experimental import pallas as pl
from jax.experimental.pallas import tpu as pltpu
from jax.sharding import PartitionSpec as P

NX = 4
NP = 32
RX = 16
BF = jnp.bfloat16
F32 = jnp.float32
LIMIT = 14 * 1024 * 1024
LARGE = 56 * 1024 * 1024

SMEM = pl.BlockSpec(memory_space=pltpu.SMEM)
VMEM = pl.BlockSpec(memory_space=pltpu.VMEM)


def whole(*shape):
    return pl.BlockSpec(shape, lambda n: (0,) * len(shape))


def params(limit=LIMIT):
    return pltpu.CompilerParams(vmem_limit_bytes=limit)


def shift(value, distance):
    return lax.ppermute(value, "prow", [(i, (i + distance) % NX) for i in range(NX)])


def around(value):
    return [value] + [shift(value, distance) for distance in range(1, NX)]


def after(value, *earlier):
    return lax.optimization_barrier((value, *earlier))[0]


def exchange(value):
    return lax.all_to_all(value, "pcol", 0, 0, tiled=True)


def reduce_columns(parts):
    return jnp.sum(exchange(parts).astype(F32), axis=0)


def gather_columns(chunk):
    chunk = chunk.astype(BF)
    return exchange(jnp.broadcast_to(chunk[None], (NP,) + chunk.shape))


def dot(left, right):
    return lax.dot_general(left, right, (((1,), (0,)), ((), ())), preferred_element_type=F32)


def dot_t(left, right):
    return lax.dot_general(left, right, (((1,), (1,)), ((), ())), preferred_element_type=F32)


def row_start(x, distance):
    return pl.multiple_of(lax.rem(x + distance, NX) * RX, RX)


def source(x, distance):
    return lax.rem(x + (NX - distance), NX)


SENT = 25


def start_kernel(place, right_sub, right_root, inverse, inverse_root, factor, lists, sent, middle, top, rights, inverses, pieces, sems):
    column = place[0]

    def copy(source_ref, target_ref, index):
        pltpu.make_async_copy(source_ref, target_ref, sems.at[index]).start()

    copy(right_sub.at[3:7], rights, 0)
    copy(inverse.at[3:7], inverses, 1)
    columns = pl.ds(pl.multiple_of(128 * column, 128), 128)
    copy(right_sub.at[0:3, :, columns], pieces.at[0:3], 4)
    copy(right_root.at[:, columns], pieces.at[3], 4)

    def factor_copy(pair, target, first, index):
        for c in range(4):
            copy(factor.at[pair, :, 128 * c : 128 * (c + 1)], target.at[first + c], index)

    for m in range(2):
        copy(inverse.at[1 + m], middle.at[m, 0:8], 2)
        for i in range(2):
            factor_copy(1 + 2 * m + i, middle.at[m], 8 + 4 * i, 2)
    copy(inverse_root, top.at[0:8], 3)
    copy(inverse.at[0], top.at[8:16], 3)
    factor_copy(0, top, 16, 3)

    names = lists[...].astype(F32).astype(BF)
    pltpu.make_async_copy(pieces, pieces, sems.at[4]).wait()
    for r in range(NX):
        sent[r, 24] = jnp.zeros((RX, 128), BF)
        sent[r, 24, 0:2, 0:17] = names
        for t in range(4):
            piece = pieces[t, RX * r : RX * (r + 1), :]
            high = piece.astype(BF)
            sent[r, 16 + t] = high
            sent[r, 20 + t] = (piece - high.astype(F32)).astype(BF)
    pltpu.make_async_copy(rights, rights, sems.at[0]).wait()
    pltpu.make_async_copy(inverses, inverses, sems.at[1]).wait()
    for n in range(4):
        own = dot(rights[n].astype(BF), inverses[n].reshape(1024, 128)).astype(BF)
        for r in range(NX):
            for g in range(NX):
                sent[r, 4 * n + g] = own[RX * g : RX * (g + 1)]
    pltpu.make_async_copy(middle, middle, sems.at[2]).wait()
    pltpu.make_async_copy(top, top, sems.at[3]).wait()


def start(place, right_sub, right_root, inverse, inverse_root, factor, lists):
    hbm = pl.BlockSpec(memory_space=pl.ANY)
    return pl.pallas_call(
        start_kernel,
        out_shape=[
            jax.ShapeDtypeStruct((NX, SENT, RX, 128), BF),
            jax.ShapeDtypeStruct((2, 16, 128, 128), BF),
            jax.ShapeDtypeStruct((20, 128, 128), BF),
        ],
        in_specs=[SMEM] + [hbm] * 5 + [VMEM],
        out_specs=[VMEM] * 3,
        scratch_shapes=[
            pltpu.VMEM((4, 64, 1024), F32),
            pltpu.VMEM((4, 8, 128, 128), BF),
            pltpu.VMEM((4, 64, 128), F32),
            pltpu.SemaphoreType.DMA((5,)),
        ],
        compiler_params=params(LARGE),
        name="start",
    )(place, right_sub, right_root, inverse, inverse_root, factor, lists)


def leaf_update_kernel(x_ref, got, inverse, f0, f1, f2, fwd, *rest):
    crit, other, packed = rest[0:4], rest[4:8], rest[8]
    x, n = x_ref[0], pl.program_id(0)

    def total(d):
        tile = 4 * n + lax.rem(x + d, NX)
        parts = [got[r, tile].astype(F32) for r in range(NX)]
        return (parts[0] + parts[1]) + (parts[2] + parts[3])

    solved = [total(d) for d in range(NX)]
    fwd[n] = solved[0]
    left = jnp.concatenate(solved, axis=0).astype(BF)
    packed[0, 0:8] = inverse[0]
    for i, factor in enumerate((f0, f1, f2)):
        first = (12, 16, 8)[i]
        for c in range(4):
            packed[0, first + c] = factor[0, :, 128 * c : 128 * (c + 1)]
        update = dot(left, factor[0]).astype(BF)
        for d in range(NX):
            piece = update[RX * d : RX * (d + 1)]
            if i == 2:
                crit[d][n] = piece
            else:
                other[d][2 * n + i] = piece


def leaf_update(x, got, inverse, factor):
    result = pl.pallas_call(
        leaf_update_kernel,
        grid=(4,),
        out_shape=[jax.ShapeDtypeStruct((4, RX, 128), F32)]
        + [jax.ShapeDtypeStruct((4, RX, 512), BF)] * 4
        + [jax.ShapeDtypeStruct((8, RX, 512), BF)] * 4
        + [jax.ShapeDtypeStruct((4, 20, 128, 128), BF)],
        in_specs=[
            SMEM,
            whole(NX, SENT, RX, 128),
            pl.BlockSpec((1, 8, 128, 128), lambda n: (3 + n, 0, 0, 0)),
        ]
        + [pl.BlockSpec((1, 128, 512), lambda n, i=i: (5 + 3 * n + i, 0, 0)) for i in range(3)],
        out_specs=[whole(4, RX, 128)]
        + [whole(4, RX, 512)] * 4
        + [whole(8, RX, 512)] * 4
        + [pl.BlockSpec((1, 20, 128, 128), lambda n: (n, 0, 0, 0))],
        compiler_params=params(LARGE),
        name="leaf_update",
    )(x, got, inverse, factor, factor, factor)
    return result[0], result[1:5], result[5:9], result[9]


def listed(table, r, pair, j):
    return table[r, j, pair]


def add_update(acc, table, r, pair, update, *lead):
    for j in range(2):
        block = listed(table, r, pair, j)
        index = (pl.ds(2 * block, 2), *lead)
        tiles = [update[:, 256 * j + 128 * h : 256 * j + 128 * (h + 1)] for h in range(2)]
        acc[index] = acc[index] + jnp.stack(tiles).astype(F32)


def leaf_spread_kernel(x_ref, table, c0, c1, c2, c3, out, acc):
    x = x_ref[0]
    acc[...] = jnp.zeros(acc.shape, F32)
    for d, crit in enumerate((c0, c1, c2, c3)):
        for n in range(4):
            add_update(acc, table, source(x, d), 5 + 3 * n + 2, crit[n], n // 2)
    out[...] = acc[...].astype(BF)


def leaf_spread(x, table, crit):
    return pl.pallas_call(
        leaf_spread_kernel,
        out_shape=jax.ShapeDtypeStruct((NP, 2, RX, 128), BF),
        in_specs=[SMEM] * 2 + [VMEM] * 4,
        scratch_shapes=[pltpu.VMEM((NP, 2, RX, 128), F32)],
        compiler_params=params(),
        name="leaf_spread",
    )(x, table, *crit)


def inverse_share(tiles):
    return tiles.reshape(1024, 128)


def factor_share(tiles):
    return jnp.concatenate([tiles[c] for c in range(4)], axis=1)


def solve_columns(values, inverse, *lead):
    total = None
    for r in range(NX):
        left = jnp.concatenate([values[(8 * r + k, *lead)] for k in range(8)], axis=1)
        term = dot(left, inverse(r))
        total = term if total is None else total + term
    return total


def solve_rows(target, inverse, store):
    for r in range(NX):
        wide = dot_t(target, inverse(r)).astype(BF)
        for k in range(8):
            store(r, k, wide[:, 128 * k : 128 * (k + 1)])


def multiply_update(acc, x, table, pair, rounded, factor, *lead):
    for r in range(NX):
        update = dot(rounded, factor(r))
        add_update(acc, table, r, pair, update, *lead)


def pick_product(x, table, pair, values, factor, *lead):
    total = None
    for r in range(NX):
        tiles = []
        for j in range(2):
            block = listed(table, r, pair, j)
            pair_of_tiles = values[(pl.ds(2 * block, 2), *lead)]
            tiles += [pair_of_tiles[0], pair_of_tiles[1]]
        term = dot_t(jnp.concatenate(tiles, axis=1), factor(r))
        total = term if total is None else total + term
    return total


TILES = whole(NP, RX, 128)
TOP_INVERSE = pl.BlockSpec((NX, 8, 128, 128), lambda n: (0, 1, 0, 0))
TOP_FACTOR = pl.BlockSpec((NX, 4, 128, 128), lambda n: (0, 4, 0, 0))


def middle_inverse(weights, m):
    return lambda r: inverse_share(weights[r, m, 0:8])


def middle_factor(weights, m, i):
    return lambda r: factor_share(weights[r, m, 8 + 4 * i : 12 + 4 * i])


def middle_forward_kernel(x_ref, table, values, weights, o0, o1, o2, o3, fwd, out, acc_root, acc):
    x = x_ref[0]
    acc[...] = jnp.zeros(acc.shape, F32)
    acc_root[...] = jnp.zeros(acc_root.shape, F32)
    for d, other in enumerate((o0, o1, o2, o3)):
        for n in range(4):
            r = source(x, d)
            add_update(acc_root, table, r, 5 + 3 * n, other[2 * n])
            add_update(acc, table, r, 5 + 3 * n + 1, other[2 * n + 1])
    for m in range(2):
        solved = solve_columns(values, middle_inverse(weights, m), m)
        fwd[m] = solved
        rounded = solved.astype(BF)
        multiply_update(acc_root, x, table, 1 + 2 * m, rounded, middle_factor(weights, m, 0))
        multiply_update(acc, x, table, 2 + 2 * m, rounded, middle_factor(weights, m, 1))
    out[...] = acc[...].astype(BF)


def middle_forward(x, table, values, weights, other):
    return pl.pallas_call(
        middle_forward_kernel,
        out_shape=[
            jax.ShapeDtypeStruct((2, RX, 128), F32),
            jax.ShapeDtypeStruct((NP, RX, 128), BF),
            jax.ShapeDtypeStruct((NP, RX, 128), F32),
        ],
        in_specs=[SMEM] * 2 + [VMEM] * 6,
        scratch_shapes=[pltpu.VMEM((NP, RX, 128), F32)],
        compiler_params=params(),
        name="middle_forward",
    )(x, table, values, weights, *other)


def top_forward_kernel(x_ref, table, values, inverse, factor, acc_in, fwd, out, acc):
    acc[...] = acc_in[...]
    solved = solve_columns(values, lambda r: inverse_share(inverse[r]))
    fwd[...] = solved
    multiply_update(
        acc, x_ref[0], table, 0, solved.astype(BF), lambda r: factor_share(factor[r])
    )
    out[...] = acc[...].astype(BF)


def top_forward(x, table, values, weights, acc_root):
    return pl.pallas_call(
        top_forward_kernel,
        grid=(1,),
        out_shape=[
            jax.ShapeDtypeStruct((RX, 128), F32),
            jax.ShapeDtypeStruct((NP, RX, 128), BF),
        ],
        in_specs=[SMEM] * 2 + [TILES, TOP_INVERSE, TOP_FACTOR, TILES],
        out_specs=[whole(RX, 128), TILES],
        scratch_shapes=[pltpu.VMEM((NP, RX, 128), F32)],
        compiler_params=params(),
        name="top_forward",
    )(x, table, values, weights, weights, acc_root)


def root_kernel(values, weights, out):
    inverse = lambda r: inverse_share(weights[r])
    rounded = solve_columns(values, inverse).astype(BF)

    def store(r, k, tile):
        out[8 * r + k] = tile

    solve_rows(rounded, inverse, store)


def root_solve(values, weights):
    return pl.pallas_call(
        root_kernel,
        grid=(1,),
        out_shape=jax.ShapeDtypeStruct((NP, RX, 128), BF),
        in_specs=[TILES, whole(NX, 8, 128, 128)],
        out_specs=TILES,
        compiler_params=params(),
        name="root_solve",
    )(values, weights)


def top_backward_kernel(x_ref, table, root, fwd, inverse, factor, out):
    down = pick_product(x_ref[0], table, 0, root, lambda r: factor_share(factor[r]))

    def store(r, k, tile):
        out[8 * r + k] = tile

    solve_rows((fwd[...] - down).astype(BF), lambda r: inverse_share(inverse[r]), store)


def top_backward(x, table, root, fwd, weights):
    return pl.pallas_call(
        top_backward_kernel,
        grid=(1,),
        out_shape=jax.ShapeDtypeStruct((NP, RX, 128), BF),
        in_specs=[SMEM] * 2 + [TILES, whole(RX, 128), TOP_INVERSE, TOP_FACTOR],
        out_specs=TILES,
        compiler_params=params(),
        name="top_backward",
    )(x, table, root, fwd, weights, weights)


def middle_backward_kernel(x_ref, table, root, top, fwd, weights, out):
    x = x_ref[0]
    for m in range(2):
        down = pick_product(x, table, 1 + 2 * m, root, middle_factor(weights, m, 0))
        down = down + pick_product(x, table, 2 + 2 * m, top, middle_factor(weights, m, 1))

        def store(r, k, tile, m=m):
            out[8 * r + k, m] = tile

        solve_rows((fwd[m] - down).astype(BF), middle_inverse(weights, m), store)


def middle_backward(x, table, root, top, fwd, weights):
    return pl.pallas_call(
        middle_backward_kernel,
        out_shape=jax.ShapeDtypeStruct((NP, 2, RX, 128), BF),
        in_specs=[SMEM] * 2 + [VMEM] * 4,
        compiler_params=params(LARGE),
        name="middle_backward",
    )(x, table, root, top, fwd, weights)


def leaf_down_kernel(x_ref, table, root, top, fwd, to_root, to_top, out):
    x = x_ref[0]
    first = 5 + 3 * pl.program_id(0)
    down = pick_product(x, table, first, root, lambda r: factor_share(to_root[r, 0]))
    down = down + pick_product(x, table, first + 1, top, lambda r: factor_share(to_top[r, 0]))
    out[0] = fwd[0] - down


def leaf_down(x, table, root, top, fwd, weights):
    factor_at = lambda i: pl.BlockSpec((NX, 1, 4, 128, 128), lambda n: (0, n, i, 0, 0))
    return pl.pallas_call(
        leaf_down_kernel,
        grid=(4,),
        out_shape=jax.ShapeDtypeStruct((4, RX, 128), F32),
        in_specs=[SMEM] * 2
        + [TILES, TILES, pl.BlockSpec((1, RX, 128), lambda n: (n, 0, 0)), factor_at(3), factor_at(4)],
        out_specs=pl.BlockSpec((1, RX, 128), lambda n: (n, 0, 0)),
        compiler_params=params(LARGE),
        name="leaf_down",
    )(x, table, root, top, fwd, weights, weights)


def leaf_backward_kernel(x_ref, table, middle, fwd, weights, out):
    x, n = x_ref[0], pl.program_id(0)
    down = pick_product(
        x, table, 7 + 3 * n, middle, lambda r: factor_share(weights[r, 0, 8:12]), n // 2
    )

    def store(r, k, tile):
        out[r, k] = tile

    inverse = lambda r: inverse_share(weights[r, 0, 0:8])
    solve_rows((fwd[0] - down).astype(BF), inverse, store)


def leaf_backward(x, table, middle, fwd, weights):
    return pl.pallas_call(
        leaf_backward_kernel,
        grid=(4,),
        out_shape=jax.ShapeDtypeStruct((NX, NP, RX, 128), BF),
        in_specs=[SMEM] * 2
        + [
            whole(NP, 2, RX, 128),
            pl.BlockSpec((1, RX, 128), lambda n: (n, 0, 0)),
            pl.BlockSpec((NX, 1, 12, 128, 128), lambda n: (0, n, 0, 0, 0)),
        ],
        out_specs=pl.BlockSpec((NX, 8, RX, 128), lambda n: (0, n, 0, 0)),
        compiler_params=params(LARGE),
        name="leaf_backward",
    )(x, table, middle, fwd, weights)


def finish_kernel(x_ref, e0, e1, e2, e3, leaves, out_sub, out_root):
    x = x_ref[0]
    for d, early in enumerate((e0, e1, e2, e3)):
        rows = pl.ds(pl.multiple_of(RX * source(x, d), RX), RX)
        for k in range(8):
            columns = slice(128 * k, 128 * (k + 1))
            out_root[rows, columns] = early[k, 0].astype(F32)
            for t in range(3):
                out_sub[t, rows, columns] = early[k, 1 + t].astype(F32)
            for t in range(4):
                tile = leaves[8 * t + k, d].astype(F32)
                out_sub[3 + t, RX * d : RX * (d + 1), columns] = tile


def finish(x, early, leaves):
    return pl.pallas_call(
        finish_kernel,
        out_shape=[
            jax.ShapeDtypeStruct((7, 64, 1024), F32),
            jax.ShapeDtypeStruct((64, 1024), F32),
        ],
        in_specs=[SMEM] + [pl.BlockSpec(memory_space=pltpu.VMEM)] * 5,
        compiler_params=params(),
        name="finish",
    )(x, *early, leaves)


def gather_rows(value):
    return lax.all_gather(value, "prow")


def per_device(right_sub, right_root, inverse_sub, inverse_root, factor_blocks, block_lists):
    position = lax.axis_index("prow").astype(jnp.int32)
    column = lax.axis_index("pcol").astype(jnp.int32)
    x = position[None]
    inverse_sub = inverse_sub.reshape(7, 8, 128, 128)
    sent, middle_weights, top_weights = start(
        (column % 8)[None],
        right_sub,
        right_root,
        inverse_sub,
        inverse_root.reshape(8, 128, 128),
        factor_blocks,
        block_lists.T,
    )
    middle_weights = gather_rows(middle_weights)

    got = lax.all_to_all(sent, "prow", 0, 0, tiled=True)
    fwd_leaf, crit, other, leaf_weights = leaf_update(x, got, inverse_sub, factor_blocks)
    crit = [crit[0]] + [shift(crit[d], d) for d in range(1, NX)]
    other = [other[0]] + [shift(other[d], d) for d in range(1, NX)]
    table = got[:, 24, 0:2, 0:17].astype(jnp.int32)
    right = lax.dynamic_index_in_dim(got, column // 8, 0, keepdims=False)
    right = right[16:20].astype(F32) + right[20:24].astype(F32)
    crit[0], right = lax.optimization_barrier((crit[0], right))
    top_weights, leaf_weights, right = lax.optimization_barrier((top_weights, leaf_weights, right))
    top_weights = gather_rows(top_weights)
    leaf_weights = gather_rows(leaf_weights)
    parts = leaf_spread(x, table, crit)

    values = gather_columns(right[1:3] - reduce_columns(parts))
    fwd_middle, parts, acc_root = middle_forward(x, table, values, middle_weights, other)
    values = gather_columns(right[0] - reduce_columns(parts))
    fwd_top, parts = top_forward(x, table, values, top_weights, acc_root)
    total = reduce_columns(parts)
    total = total + lax.ppermute(total, "layer", [(0, 1), (1, 0)])
    values = gather_columns(right[3] - total)
    root = gather_columns(reduce_columns(root_solve(values, top_weights)))
    parts = top_backward(x, table, root, fwd_top, top_weights)
    top = gather_columns(reduce_columns(parts))
    parts = middle_backward(x, table, root, top, fwd_middle, middle_weights)
    fwd_leaf = leaf_down(x, table, root, top, fwd_leaf, leaf_weights)
    middle = gather_columns(reduce_columns(parts))

    early = jnp.concatenate([root[:, None], top[:, None], middle], 1)
    pieces = []
    for d in range(NX):
        piece = lax.dynamic_slice_in_dim(early, 8 * lax.rem(position + d, NX), 8, 0)
        pieces.append(shift(piece, d) if d else piece)

    parts = leaf_backward(x, table, middle, fwd_leaf, leaf_weights)
    parts = lax.all_to_all(
        parts.reshape(NX * NP, RX, 128), ("prow", "pcol"), 0, 0, tiled=True
    ).reshape(NX, NP, RX, 128)
    chunk = jnp.sum(parts.astype(F32), axis=1).astype(BF)
    leaves = gather_columns(after(chunk, *pieces))
    return tuple(finish(x, pieces, leaves))


def solution(mesh):
    in_specs = (
        P("layer", None, "prow"),
        P(None, "prow"),
        P("layer", "prow", "pcol"),
        P("prow", "pcol"),
        P("layer", "pcol", "prow"),
        P("layer", "prow"),
    )
    out_specs = (P("layer", None, "prow"), P(None, "prow"))
    return jax.shard_map(
        per_device, mesh=mesh, in_specs=in_specs, out_specs=out_specs, check_vma=False
    )
```

```python
import jax
import jax.numpy as jnp
from jax import lax
from jax.experimental import pallas as pl
from jax.experimental.pallas import tpu as pltpu
from jax.sharding import PartitionSpec as P

NX = 4
NP = 32
RX = 16
BF = jnp.bfloat16
F32 = jnp.float32
LIMIT = 14 * 1024 * 1024
LARGE = 56 * 1024 * 1024

SMEM = pl.BlockSpec(memory_space=pltpu.SMEM)
VMEM = pl.BlockSpec(memory_space=pltpu.VMEM)


def whole(*shape):
    return pl.BlockSpec(shape, lambda n: (0,) * len(shape))


def params(limit=LIMIT):
    return pltpu.CompilerParams(vmem_limit_bytes=limit)


def shift(value, distance):
    return lax.ppermute(value, "prow", [(i, (i + distance) % NX) for i in range(NX)])


def around(value):
    return [value] + [shift(value, distance) for distance in range(1, NX)]


def after(value, *earlier):
    return lax.optimization_barrier((value, *earlier))[0]


def exchange(value):
    return lax.all_to_all(value, "pcol", 0, 0, tiled=True)


def reduce_columns(parts):
    return jnp.sum(exchange(parts).astype(F32), axis=0)


def gather_columns(chunk):
    chunk = chunk.astype(BF)
    return exchange(jnp.broadcast_to(chunk[None], (NP,) + chunk.shape))


def dot(left, right):
    return lax.dot_general(left, right, (((1,), (0,)), ((), ())), preferred_element_type=F32)


def dot_t(left, right):
    return lax.dot_general(left, right, (((1,), (1,)), ((), ())), preferred_element_type=F32)


def row_start(x, distance):
    return pl.multiple_of(lax.rem(x + distance, NX) * RX, RX)


def source(x, distance):
    return lax.rem(x + (NX - distance), NX)


SENT = 25


def start_kernel(place, right_sub, right_root, inverse, inverse_root, factor, lists, sent, middle, top, rights, inverses, pieces, sems):
    column = place[0]

    def copy(source_ref, target_ref, index):
        pltpu.make_async_copy(source_ref, target_ref, sems.at[index]).start()

    copy(right_sub.at[3:7], rights, 0)
    copy(inverse.at[3:7], inverses, 1)
    columns = pl.ds(pl.multiple_of(128 * column, 128), 128)
    copy(right_sub.at[0:3, :, columns], pieces.at[0:3], 4)
    copy(right_root.at[:, columns], pieces.at[3], 4)

    def factor_copy(pair, target, first, index):
        for c in range(4):
            copy(factor.at[pair, :, 128 * c : 128 * (c + 1)], target.at[first + c], index)

    for m in range(2):
        copy(inverse.at[1 + m], middle.at[m, 0:8], 2)
        for i in range(2):
            factor_copy(1 + 2 * m + i, middle.at[m], 8 + 4 * i, 2)
    copy(inverse_root, top.at[0:8], 3)
    copy(inverse.at[0], top.at[8:16], 3)
    factor_copy(0, top, 16, 3)

    names = lists[...].astype(F32).astype(BF)
    pltpu.make_async_copy(pieces, pieces, sems.at[4]).wait()
    for r in range(NX):
        sent[r, 24] = jnp.zeros((RX, 128), BF)
        sent[r, 24, 0:2, 0:17] = names
        for t in range(4):
            piece = pieces[t, RX * r : RX * (r + 1), :]
            high = piece.astype(BF)
            sent[r, 16 + t] = high
            sent[r, 20 + t] = (piece - high.astype(F32)).astype(BF)
    pltpu.make_async_copy(rights, rights, sems.at[0]).wait()
    pltpu.make_async_copy(inverses, inverses, sems.at[1]).wait()
    for n in range(4):
        own = dot(rights[n].astype(BF), inverses[n].reshape(1024, 128)).astype(BF)
        for r in range(NX):
            for g in range(NX):
                sent[r, 4 * n + g] = own[RX * g : RX * (g + 1)]
    pltpu.make_async_copy(middle, middle, sems.at[2]).wait()
    pltpu.make_async_copy(top, top, sems.at[3]).wait()


def start(place, right_sub, right_root, inverse, inverse_root, factor, lists):
    hbm = pl.BlockSpec(memory_space=pl.ANY)
    return pl.pallas_call(
        start_kernel,
        out_shape=[
            jax.ShapeDtypeStruct((NX, SENT, RX, 128), BF),
            jax.ShapeDtypeStruct((2, 16, 128, 128), BF),
            jax.ShapeDtypeStruct((20, 128, 128), BF),
        ],
        in_specs=[SMEM] + [hbm] * 5 + [VMEM],
        out_specs=[VMEM] * 3,
        scratch_shapes=[
            pltpu.VMEM((4, 64, 1024), F32),
            pltpu.VMEM((4, 8, 128, 128), BF),
            pltpu.VMEM((4, 64, 128), F32),
            pltpu.SemaphoreType.DMA((5,)),
        ],
        compiler_params=params(LARGE),
        name="start",
    )(place, right_sub, right_root, inverse, inverse_root, factor, lists)


def leaf_update_kernel(x_ref, got, inverse, f0, f1, f2, fwd, *rest):
    crit, other, packed = rest[0:4], rest[4:8], rest[8]
    x, n = x_ref[0], pl.program_id(0)

    def total(d):
        tile = 4 * n + lax.rem(x + d, NX)
        parts = [got[r, tile].astype(F32) for r in range(NX)]
        return (parts[0] + parts[1]) + (parts[2] + parts[3])

    solved = [total(d) for d in range(NX)]
    fwd[n] = solved[0]
    left = jnp.concatenate(solved, axis=0).astype(BF)
    packed[0, 0:8] = inverse[0]
    for i, factor in enumerate((f0, f1, f2)):
        first = (12, 16, 8)[i]
        for c in range(4):
            packed[0, first + c] = factor[0, :, 128 * c : 128 * (c + 1)]
        update = dot(left, factor[0]).astype(BF)
        for d in range(NX):
            piece = update[RX * d : RX * (d + 1)]
            if i == 2:
                crit[d][n] = piece
            else:
                other[d][2 * n + i] = piece


def leaf_update(x, got, inverse, factor):
    result = pl.pallas_call(
        leaf_update_kernel,
        grid=(4,),
        out_shape=[jax.ShapeDtypeStruct((4, RX, 128), F32)]
        + [jax.ShapeDtypeStruct((4, RX, 512), BF)] * 4
        + [jax.ShapeDtypeStruct((8, RX, 512), BF)] * 4
        + [jax.ShapeDtypeStruct((4, 20, 128, 128), BF)],
        in_specs=[
            SMEM,
            whole(NX, SENT, RX, 128),
            pl.BlockSpec((1, 8, 128, 128), lambda n: (3 + n, 0, 0, 0)),
        ]
        + [pl.BlockSpec((1, 128, 512), lambda n, i=i: (5 + 3 * n + i, 0, 0)) for i in range(3)],
        out_specs=[whole(4, RX, 128)]
        + [whole(4, RX, 512)] * 4
        + [whole(8, RX, 512)] * 4
        + [pl.BlockSpec((1, 20, 128, 128), lambda n: (n, 0, 0, 0))],
        compiler_params=params(LARGE),
        name="leaf_update",
    )(x, got, inverse, factor, factor, factor)
    return result[0], result[1:5], result[5:9], result[9]


def listed(table, r, pair, j):
    return table[r, j, pair]


def add_update(acc, table, r, pair, update, *lead):
    for j in range(2):
        block = listed(table, r, pair, j)
        index = (pl.ds(2 * block, 2), *lead)
        tiles = [update[:, 256 * j + 128 * h : 256 * j + 128 * (h + 1)] for h in range(2)]
        acc[index] = acc[index] + jnp.stack(tiles).astype(F32)


def leaf_spread_kernel(x_ref, table, c0, c1, c2, c3, out, acc):
    x = x_ref[0]
    acc[...] = jnp.zeros(acc.shape, F32)
    for d, crit in enumerate((c0, c1, c2, c3)):
        for n in range(4):
            add_update(acc, table, source(x, d), 5 + 3 * n + 2, crit[n], n // 2)
    out[...] = acc[...].astype(BF)


def leaf_spread(x, table, crit):
    return pl.pallas_call(
        leaf_spread_kernel,
        out_shape=jax.ShapeDtypeStruct((NP, 2, RX, 128), BF),
        in_specs=[SMEM] * 2 + [VMEM] * 4,
        scratch_shapes=[pltpu.VMEM((NP, 2, RX, 128), F32)],
        compiler_params=params(),
        name="leaf_spread",
    )(x, table, *crit)


def inverse_share(tiles):
    return tiles.reshape(1024, 128)


def factor_share(tiles):
    return jnp.concatenate([tiles[c] for c in range(4)], axis=1)


def solve_columns(values, inverse, *lead):
    total = None
    for r in range(NX):
        left = jnp.concatenate([values[(8 * r + k, *lead)] for k in range(8)], axis=1)
        term = dot(left, inverse(r))
        total = term if total is None else total + term
    return total


def solve_rows(target, inverse, store):
    for r in range(NX):
        wide = dot_t(target, inverse(r)).astype(BF)
        for k in range(8):
            store(r, k, wide[:, 128 * k : 128 * (k + 1)])


def multiply_update(acc, x, table, pair, rounded, factor, *lead):
    for r in range(NX):
        update = dot(rounded, factor(r))
        add_update(acc, table, r, pair, update, *lead)


def pick_product(x, table, pair, values, factor, *lead):
    total = None
    for r in range(NX):
        tiles = []
        for j in range(2):
            block = listed(table, r, pair, j)
            pair_of_tiles = values[(pl.ds(2 * block, 2), *lead)]
            tiles += [pair_of_tiles[0], pair_of_tiles[1]]
        term = dot_t(jnp.concatenate(tiles, axis=1), factor(r))
        total = term if total is None else total + term
    return total


TILES = whole(NP, RX, 128)
TOP_INVERSE = pl.BlockSpec((NX, 8, 128, 128), lambda n: (0, 1, 0, 0))
TOP_FACTOR = pl.BlockSpec((NX, 4, 128, 128), lambda n: (0, 4, 0, 0))


def middle_inverse(weights, m):
    return lambda r: inverse_share(weights[r, m, 0:8])


def middle_factor(weights, m, i):
    return lambda r: factor_share(weights[r, m, 8 + 4 * i : 12 + 4 * i])


def middle_forward_kernel(x_ref, table, values, weights, o0, o1, o2, o3, fwd, out, acc_root, acc):
    x = x_ref[0]
    acc[...] = jnp.zeros(acc.shape, F32)
    acc_root[...] = jnp.zeros(acc_root.shape, F32)
    for d, other in enumerate((o0, o1, o2, o3)):
        for n in range(4):
            r = source(x, d)
            add_update(acc_root, table, r, 5 + 3 * n, other[2 * n])
            add_update(acc, table, r, 5 + 3 * n + 1, other[2 * n + 1])
    for m in range(2):
        solved = solve_columns(values, middle_inverse(weights, m), m)
        fwd[m] = solved
        rounded = solved.astype(BF)
        multiply_update(acc_root, x, table, 1 + 2 * m, rounded, middle_factor(weights, m, 0))
        multiply_update(acc, x, table, 2 + 2 * m, rounded, middle_factor(weights, m, 1))
    out[...] = acc[...].astype(BF)


def middle_forward(x, table, values, weights, other):
    return pl.pallas_call(
        middle_forward_kernel,
        out_shape=[
            jax.ShapeDtypeStruct((2, RX, 128), F32),
            jax.ShapeDtypeStruct((NP, RX, 128), BF),
            jax.ShapeDtypeStruct((NP, RX, 128), F32),
        ],
        in_specs=[SMEM] * 2 + [VMEM] * 6,
        scratch_shapes=[pltpu.VMEM((NP, RX, 128), F32)],
        compiler_params=params(),
        name="middle_forward",
    )(x, table, values, weights, *other)


def top_forward_kernel(x_ref, table, values, inverse, factor, acc_in, fwd, out, acc):
    acc[...] = acc_in[...]
    solved = solve_columns(values, lambda r: inverse_share(inverse[r]))
    fwd[...] = solved
    multiply_update(
        acc, x_ref[0], table, 0, solved.astype(BF), lambda r: factor_share(factor[r])
    )
    out[...] = acc[...].astype(BF)


def top_forward(x, table, values, weights, acc_root):
    return pl.pallas_call(
        top_forward_kernel,
        grid=(1,),
        out_shape=[
            jax.ShapeDtypeStruct((RX, 128), F32),
            jax.ShapeDtypeStruct((NP, RX, 128), BF),
        ],
        in_specs=[SMEM] * 2 + [TILES, TOP_INVERSE, TOP_FACTOR, TILES],
        out_specs=[whole(RX, 128), TILES],
        scratch_shapes=[pltpu.VMEM((NP, RX, 128), F32)],
        compiler_params=params(),
        name="top_forward",
    )(x, table, values, weights, weights, acc_root)


def root_kernel(values, weights, out):
    inverse = lambda r: inverse_share(weights[r])
    rounded = solve_columns(values, inverse).astype(BF)

    def store(r, k, tile):
        out[8 * r + k] = tile

    solve_rows(rounded, inverse, store)


def root_solve(values, weights):
    return pl.pallas_call(
        root_kernel,
        grid=(1,),
        out_shape=jax.ShapeDtypeStruct((NP, RX, 128), BF),
        in_specs=[TILES, whole(NX, 8, 128, 128)],
        out_specs=TILES,
        compiler_params=params(),
        name="root_solve",
    )(values, weights)


def top_backward_kernel(x_ref, table, root, fwd, inverse, factor, out):
    down = pick_product(x_ref[0], table, 0, root, lambda r: factor_share(factor[r]))

    def store(r, k, tile):
        out[8 * r + k] = tile

    solve_rows((fwd[...] - down).astype(BF), lambda r: inverse_share(inverse[r]), store)


def top_backward(x, table, root, fwd, weights):
    return pl.pallas_call(
        top_backward_kernel,
        grid=(1,),
        out_shape=jax.ShapeDtypeStruct((NP, RX, 128), BF),
        in_specs=[SMEM] * 2 + [TILES, whole(RX, 128), TOP_INVERSE, TOP_FACTOR],
        out_specs=TILES,
        compiler_params=params(),
        name="top_backward",
    )(x, table, root, fwd, weights, weights)


def middle_backward_kernel(x_ref, table, root, top, fwd, weights, out):
    x = x_ref[0]
    for m in range(2):
        down = pick_product(x, table, 1 + 2 * m, root, middle_factor(weights, m, 0))
        down = down + pick_product(x, table, 2 + 2 * m, top, middle_factor(weights, m, 1))

        def store(r, k, tile, m=m):
            out[8 * r + k, m] = tile

        solve_rows((fwd[m] - down).astype(BF), middle_inverse(weights, m), store)


def middle_backward(x, table, root, top, fwd, weights):
    return pl.pallas_call(
        middle_backward_kernel,
        out_shape=jax.ShapeDtypeStruct((NP, 2, RX, 128), BF),
        in_specs=[SMEM] * 2 + [VMEM] * 4,
        compiler_params=params(LARGE),
        name="middle_backward",
    )(x, table, root, top, fwd, weights)


def leaf_down_kernel(x_ref, table, root, top, fwd, to_root, to_top, out):
    x = x_ref[0]
    first = 5 + 3 * pl.program_id(0)
    down = pick_product(x, table, first, root, lambda r: factor_share(to_root[r, 0]))
    down = down + pick_product(x, table, first + 1, top, lambda r: factor_share(to_top[r, 0]))
    out[0] = fwd[0] - down


def leaf_down(x, table, root, top, fwd, weights):
    factor_at = lambda i: pl.BlockSpec((NX, 1, 4, 128, 128), lambda n: (0, n, i, 0, 0))
    return pl.pallas_call(
        leaf_down_kernel,
        grid=(4,),
        out_shape=jax.ShapeDtypeStruct((4, RX, 128), F32),
        in_specs=[SMEM] * 2
        + [TILES, TILES, pl.BlockSpec((1, RX, 128), lambda n: (n, 0, 0)), factor_at(3), factor_at(4)],
        out_specs=pl.BlockSpec((1, RX, 128), lambda n: (n, 0, 0)),
        compiler_params=params(LARGE),
        name="leaf_down",
    )(x, table, root, top, fwd, weights, weights)


def leaf_backward_kernel(x_ref, table, middle, fwd, weights, out):
    x, n = x_ref[0], pl.program_id(0)
    down = pick_product(
        x, table, 7 + 3 * n, middle, lambda r: factor_share(weights[r, 0, 8:12]), n // 2
    )

    def store(r, k, tile):
        out[r, k] = tile

    inverse = lambda r: inverse_share(weights[r, 0, 0:8])
    solve_rows((fwd[0] - down).astype(BF), inverse, store)


def leaf_backward(x, table, middle, fwd, weights):
    return pl.pallas_call(
        leaf_backward_kernel,
        grid=(4,),
        out_shape=jax.ShapeDtypeStruct((NX, NP, RX, 128), BF),
        in_specs=[SMEM] * 2
        + [
            whole(NP, 2, RX, 128),
            pl.BlockSpec((1, RX, 128), lambda n: (n, 0, 0)),
            pl.BlockSpec((NX, 1, 12, 128, 128), lambda n: (0, n, 0, 0, 0)),
        ],
        out_specs=pl.BlockSpec((NX, 8, RX, 128), lambda n: (0, n, 0, 0)),
        compiler_params=params(LARGE),
        name="leaf_backward",
    )(x, table, middle, fwd, weights)


def finish_kernel(x_ref, *refs):
    upper, middle, (leaves, out_sub, out_root) = refs[0:4], refs[4:8], refs[8:]
    x = x_ref[0]
    for d in range(NX):
        rows = pl.ds(pl.multiple_of(RX * source(x, d), RX), RX)
        for k in range(8):
            columns = slice(128 * k, 128 * (k + 1))
            out_root[rows, columns] = upper[d][k, 0].astype(F32)
            out_sub[0, rows, columns] = upper[d][k, 1].astype(F32)
            for t in range(2):
                out_sub[1 + t, rows, columns] = middle[d][k, t].astype(F32)
            for t in range(4):
                tile = leaves[8 * t + k, d].astype(F32)
                out_sub[3 + t, RX * d : RX * (d + 1), columns] = tile


def finish(x, upper, middle, leaves):
    return pl.pallas_call(
        finish_kernel,
        out_shape=[
            jax.ShapeDtypeStruct((7, 64, 1024), F32),
            jax.ShapeDtypeStruct((64, 1024), F32),
        ],
        in_specs=[SMEM] + [VMEM] * 9,
        compiler_params=params(),
        name="finish",
    )(x, *upper, *middle, leaves)


def gather_rows(value):
    return lax.all_gather(value, "prow")


def per_device(right_sub, right_root, inverse_sub, inverse_root, factor_blocks, block_lists):
    position = lax.axis_index("prow").astype(jnp.int32)
    column = lax.axis_index("pcol").astype(jnp.int32)
    x = position[None]
    inverse_sub = inverse_sub.reshape(7, 8, 128, 128)
    sent, middle_weights, top_weights = start(
        (column % 8)[None],
        right_sub,
        right_root,
        inverse_sub,
        inverse_root.reshape(8, 128, 128),
        factor_blocks,
        block_lists.T,
    )
    middle_weights = gather_rows(middle_weights)

    got = lax.all_to_all(sent, "prow", 0, 0, tiled=True)
    fwd_leaf, crit, other, leaf_weights = leaf_update(x, got, inverse_sub, factor_blocks)
    crit = [crit[0]] + [shift(crit[d], d) for d in range(1, NX)]
    other = [other[0]] + [shift(other[d], d) for d in range(1, NX)]
    table = got[:, 24, 0:2, 0:17].astype(jnp.int32)
    right = lax.dynamic_index_in_dim(got, column // 8, 0, keepdims=False)
    right = right[16:20].astype(F32) + right[20:24].astype(F32)
    crit[0], right = lax.optimization_barrier((crit[0], right))
    top_weights, leaf_weights, right = lax.optimization_barrier((top_weights, leaf_weights, right))
    top_weights = gather_rows(top_weights)
    leaf_weights = gather_rows(leaf_weights)
    parts = leaf_spread(x, table, crit)

    values = gather_columns(right[1:3] - reduce_columns(parts))
    fwd_middle, parts, acc_root = middle_forward(x, table, values, middle_weights, other)
    values = gather_columns(right[0] - reduce_columns(parts))
    fwd_top, parts = top_forward(x, table, values, top_weights, acc_root)
    total = reduce_columns(parts)
    total = total + lax.ppermute(total, "layer", [(0, 1), (1, 0)])
    values = gather_columns(right[3] - total)
    root = gather_columns(reduce_columns(root_solve(values, top_weights)))
    parts = top_backward(x, table, root, fwd_top, top_weights)
    top = gather_columns(reduce_columns(parts))
    parts = middle_backward(x, table, root, top, fwd_middle, middle_weights)
    fwd_leaf = leaf_down(x, table, root, top, fwd_leaf, leaf_weights)
    middle = gather_columns(reduce_columns(parts))

    def own_columns(values):
        found = []
        for d in range(NX):
            piece = lax.dynamic_slice_in_dim(values, 8 * lax.rem(position + d, NX), 8, 0)
            found.append(shift(piece, d) if d else piece)
        return found

    upper = own_columns(jnp.stack([root, top], 1))
    fwd_leaf, *upper = lax.optimization_barrier((fwd_leaf, *upper))
    pieces = own_columns(middle)
    parts = leaf_backward(x, table, middle, fwd_leaf, leaf_weights)
    parts = lax.all_to_all(
        parts.reshape(NX * NP, RX, 128), ("prow", "pcol"), 0, 0, tiled=True
    ).reshape(NX, NP, RX, 128)
    chunk = jnp.sum(parts.astype(F32), axis=1).astype(BF)
    leaves = gather_columns(after(chunk, *pieces))
    return tuple(finish(x, upper, pieces, leaves))


def solution(mesh):
    in_specs = (
        P("layer", None, "prow"),
        P(None, "prow"),
        P("layer", "prow", "pcol"),
        P("prow", "pcol"),
        P("layer", "pcol", "prow"),
        P("layer", "prow"),
    )
    out_specs = (P("layer", None, "prow"), P(None, "prow"))
    return jax.shard_map(
        per_device, mesh=mesh, in_specs=in_specs, out_specs=out_specs, check_vma=False
    )
```
